32 devices in a mesh: groups: 2 (over y), ctx: 4 (over z), tp: 4 (over x, core).
Axes of the slice: x: 2, y: 2, z: 4, core: 2. Of those that a mesh axis runs over, the one named last changes fastest.
Arguments:
- hidden: bfloat16 [1024, 8192], P(('groups', 'ctx'), 'tp'), parts along dimension 0, may hold values from -6 to 6
- base_query_rows: bfloat16 [1024, 8192], P(('groups', 'ctx'), 'tp'), parts along dimension 0, may hold values from -60 to 60
- base_key_rows: bfloat16 [1024, 1024], P(('groups', 'ctx'), 'tp'), parts along dimension 0, may hold values from -60 to 60
- base_value_rows: bfloat16 [1024, 1024], P(('groups', 'ctx'), 'tp'), parts along dimension 0, may hold values from -6 to 6
- stored_block_order: int32 [16], P('groups'), parts along dimension 0, may hold values from 0 to 7, each once
- version: int32 [8], P('groups'), parts along dimension 0, may hold values from 0 to 3
- publisher: int32 [2], P('groups'), parts along dimension 0, may hold values from 0 to 3
- adapter_down_weight: bfloat16 [4, 4, 192, 8192], P('ctx', None, None, 'tp'), may hold values from -0.0625 to 0.0625
- adapter_up_query: bfloat16 [4, 4, 64, 8192], P('ctx', None, None, 'tp'), may hold values from -0.75 to 0.75
- adapter_up_key_value: bfloat16 [4, 4, 2, 64, 1024], P('ctx', None, None, None, 'tp'), may hold values from -0.75 to 0.75
- output_down_weight: bfloat16 [4, 4, 64, 8192], P('ctx', None, None, 'tp'), may hold values from -0.1875 to 0.1875
- output_up_weight: bfloat16 [4, 4, 64, 8192], P('ctx', None, None, 'tp'), may hold values from -0.75 to 0.75
Outputs:
- attended: bfloat16 [1024, 8192], P(('groups', 'ctx'), 'tp'), parts along dimension 0
- adapted: bfloat16 [1024, 8192], P(('groups', 'ctx'), 'tp'), parts along dimension 0
The draws below stay inside these ranges and needn't reach their ends.
There are 2 independent parts, one for each index of `groups`. The reference program is written for one: setup_inputs(seed, part) draws one part's arguments, and reference() takes and returns one part's arrays. A program takes and returns all parts, laid end to end along the dimension named above; an argument that names none is the same for every part. Nothing has to cross between parts.
Inputs may be any that keep to these rules, and one draw needn't show every extreme that they name: `stored_block_order`: each half-block of the prompt is stored exactly once.
All inputs are finite; a program needn't handle non-finite values.
Results may differ from the reference program's by a relative error of at most 0.015.
The reference program's roundings to bfloat16 on the way count: a program that leaves them out, or rounds other values in their place, can miss the bound.
Values may be sent and summed in bfloat16 or wider, within the bound.
No kernel may reach another device: no remote copies, remote signals or barrier semaphores. Data moves between devices by JAX's collectives and lax.ppermute only.
A program may use at most 64 MiB of HBM per device.

```python
import jax
import jax.numpy as jnp
from jax import lax

MODEL_WIDTH = 8192
QUERY_HEADS = 64
KEY_VALUE_HEADS = 8
HEAD_SIZE = 128
ADAPTER_RANK = 64
SLOT_VERSIONS = 4
PROMPT_TOKENS = 512
HBLK = 64
BLOCKS = 8
N_CTX = 4


def draw_base_query_rows(key, part):
    base_output = jnp.clip(1.6 * jax.random.normal(jax.random.fold_in(key, 11), (PROMPT_TOKENS, QUERY_HEADS, HEAD_SIZE), jnp.float32), -9.0, 9.0)
    return base_output.reshape(PROMPT_TOKENS, QUERY_HEADS * HEAD_SIZE).astype(jnp.bfloat16)


def draw_base_key_rows(key, part):
    base_output = jnp.clip(1.6 * jax.random.normal(jax.random.fold_in(key, 21), (PROMPT_TOKENS, KEY_VALUE_HEADS, HEAD_SIZE), jnp.float32), -9.0, 9.0)
    return base_output.reshape(PROMPT_TOKENS, KEY_VALUE_HEADS * HEAD_SIZE).astype(jnp.bfloat16)


def touch_ends(entries, key, low, high):
    shape = entries.shape
    spot = [jax.random.randint(jax.random.fold_in(key, axis), (), 0, shape[axis]) for axis in range(len(shape))]
    entries = entries.at[tuple(spot)].set(low)
    longest = shape.index(max(shape))
    spot[longest] = (spot[longest] + 1) % shape[longest]
    return entries.at[tuple(spot)].set(high)


def levels(own_key, dims, shards, low, high):
    def one(position, blocks):
        draws = jax.random.uniform(jax.random.fold_in(jax.random.fold_in(own_key, 6), position), (blocks,), jnp.float32, low / len(shards), high / len(shards))
        return jnp.repeat(jnp.exp(draws), dims[position] // blocks).reshape((-1,) + (1,) * (len(dims) - position - 1))

    gain = one(*shards[0])
    for cut in shards[1:]:
        gain = gain * one(*cut)
    return gain


def bell_draw(own_key, extent, scale, bound, split=(), kind=jnp.bfloat16):
    result = jax.random.normal(own_key, extent, jnp.float32) * scale
    if len(split) > 0:
        result = levels(own_key, extent, split, -0.22, 0.18) * result
    return jnp.clip(result, min=-bound, max=bound).astype(kind)


def setup_inputs(seed: int = 0, part: int = 0) -> dict:
    key_of = jax.random.split(jax.random.key(seed), 13)
    part_keys = jax.random.split(jax.random.fold_in(key_of[12], part), 13)
    return {
        "hidden": bell_draw(part_keys[0], (PROMPT_TOKENS, MODEL_WIDTH), 1.0, 6.0, ((0, 4), (1, 4))),
        "base_query_rows": draw_base_query_rows(jax.random.fold_in(jax.random.fold_in(key_of[12], part), 71), part),
        "base_key_rows": draw_base_key_rows(jax.random.fold_in(jax.random.fold_in(key_of[12], part), 71), part),
        "base_value_rows": bell_draw(part_keys[3], (PROMPT_TOKENS, KEY_VALUE_HEADS * HEAD_SIZE), 1.0, 6.0, ((0, 4), (1, 4))),
        "stored_block_order": jax.random.permutation(part_keys[4], BLOCKS).astype(jnp.int32),
        "version": touch_ends(jax.random.randint(part_keys[5], (N_CTX,), 0, SLOT_VERSIONS), jax.random.fold_in(part_keys[5], 1), 0, SLOT_VERSIONS - 1).astype(jnp.int32),
        "publisher": jax.random.randint(part_keys[6], (1,), 0, N_CTX).astype(jnp.int32),
        "adapter_down_weight": bell_draw(key_of[7], (N_CTX, SLOT_VERSIONS, 3 * ADAPTER_RANK, MODEL_WIDTH), MODEL_WIDTH ** -0.5, 0.0625, ((0, 4), (3, 4))),
        "adapter_up_query": bell_draw(key_of[8], (N_CTX, SLOT_VERSIONS, ADAPTER_RANK, QUERY_HEADS * HEAD_SIZE), ADAPTER_RANK ** -0.5, 0.75, ((0, 4), (3, 4))),
        "adapter_up_key_value": bell_draw(key_of[9], (N_CTX, SLOT_VERSIONS, 2, ADAPTER_RANK, KEY_VALUE_HEADS * HEAD_SIZE), ADAPTER_RANK ** -0.5, 0.75, ((0, 4), (4, 4))),
        "output_down_weight": bell_draw(key_of[10], (N_CTX, SLOT_VERSIONS, ADAPTER_RANK, QUERY_HEADS * HEAD_SIZE), (QUERY_HEADS * HEAD_SIZE // 8) ** -0.5, 0.1875, ((0, 4), (3, 4))),
        "output_up_weight": bell_draw(key_of[11], (N_CTX, SLOT_VERSIONS, ADAPTER_RANK, MODEL_WIDTH), ADAPTER_RANK ** -0.5, 0.75, ((0, 4), (3, 4))),
    }


NEG_BIG = -1.0e30


def apply_rotation(values, token_index_list):
    half_dim = values.shape[-1] // 2
    frequency = 500000.0 ** (-(jnp.arange(half_dim, dtype=jnp.float32) * 2.0) / values.shape[-1])
    angles = token_index_list.astype(jnp.float32)[:, None] * frequency[None, :]
    cosine = jnp.cos(angles)[:, None, :]
    sine_part = jnp.sin(angles)[:, None, :]
    first_half = values[..., :half_dim]
    second_half = values[..., half_dim:]
    return jnp.concatenate([first_half * cosine - second_half * sine_part, second_half * cosine + first_half * sine_part], axis=-1)


def token_positions(stored_block_order):
    flat_index = jnp.arange(PROMPT_TOKENS, dtype=jnp.int32)
    return stored_block_order[flat_index // HBLK] * HBLK + flat_index % HBLK


def reference(hidden, base_query_rows, base_key_rows, base_value_rows, stored_block_order, version, publisher, adapter_down_weight, adapter_up_query, adapter_up_key_value, output_down_weight, output_up_weight):
    source_block = publisher[0]
    chosen_version = version[source_block]
    down_output = adapter_down_weight[source_block, chosen_version]
    rank_projection = jnp.dot(hidden, down_output.T, preferred_element_type=jnp.float32).astype(jnp.bfloat16)
    token_index_list = token_positions(stored_block_order)
    adapted_queries = base_query_rows.astype(jnp.float32) + jnp.dot(rank_projection[:, :ADAPTER_RANK], adapter_up_query[source_block, chosen_version], preferred_element_type=jnp.float32)
    adapted_queries = apply_rotation(adapted_queries.reshape(PROMPT_TOKENS, QUERY_HEADS, HEAD_SIZE), token_index_list).astype(jnp.bfloat16)
    adapted_key_rows = base_key_rows.astype(jnp.float32) + jnp.dot(rank_projection[:, ADAPTER_RANK:2 * ADAPTER_RANK], adapter_up_key_value[source_block, chosen_version, 0], preferred_element_type=jnp.float32)
    adapted_key_rows = apply_rotation(adapted_key_rows.reshape(PROMPT_TOKENS, KEY_VALUE_HEADS, HEAD_SIZE), token_index_list).astype(jnp.bfloat16)
    adapted_value_rows = base_value_rows.astype(jnp.float32) + jnp.dot(rank_projection[:, 2 * ADAPTER_RANK:], adapter_up_key_value[source_block, chosen_version, 1], preferred_element_type=jnp.float32)
    adapted_value_rows = adapted_value_rows.astype(jnp.bfloat16).reshape(PROMPT_TOKENS, KEY_VALUE_HEADS, HEAD_SIZE)
    query_group_size = QUERY_HEADS // KEY_VALUE_HEADS
    head_queries = jnp.transpose(adapted_queries, (1, 0, 2))
    head_keys = jnp.repeat(jnp.transpose(adapted_key_rows, (1, 0, 2)), query_group_size, axis=0)
    head_values = jnp.repeat(jnp.transpose(adapted_value_rows, (1, 0, 2)), query_group_size, axis=0)
    visible = token_index_list[None, :] <= token_index_list[:, None]

    def one_head(operands):
        query_head, key_head, value_head = operands
        scores = jnp.dot(query_head, key_head.T, preferred_element_type=jnp.float32) * (HEAD_SIZE ** -0.5)
        scores = jnp.where(visible, scores, NEG_BIG)
        row_max = jnp.max(scores, axis=1, keepdims=True)
        raw_scores = jnp.where(visible, jnp.exp(scores - row_max), 0.0)
        totals = jnp.sum(raw_scores, axis=1)
        mixed = jnp.dot(raw_scores.astype(jnp.bfloat16), value_head, preferred_element_type=jnp.float32)
        return (mixed / totals[:, None]).astype(jnp.bfloat16)

    attended = lax.map(one_head, (head_queries, head_keys, head_values))
    attended = jnp.transpose(attended, (1, 0, 2)).reshape(PROMPT_TOKENS, QUERY_HEADS * HEAD_SIZE)
    out_low = jnp.dot(attended, output_down_weight[source_block, chosen_version].T, preferred_element_type=jnp.float32).astype(jnp.bfloat16)
    adapted = jnp.dot(out_low, output_up_weight[source_block, chosen_version], preferred_element_type=jnp.float32).astype(jnp.bfloat16)
    return attended, adapted
```

```python
import jax
import jax.numpy as jnp
from jax import lax
from jax.sharding import PartitionSpec as P

HEAD_SIZE = 128
ADAPTER_RANK = 64
NEG_BIG = -1e30
CHUNK_ROWS = 32
LAG = 2


def after(value, *earlier):
    return lax.optimization_barrier((value,) + earlier)[0]


def ring_order(count):
    return [0] + list(range(1, count, 2)) + list(range(2, count, 2))[::-1]


def ring_place(index, count):
    table = [0] * count
    for place, member in enumerate(ring_order(count)):
        table[member] = place
    place = jnp.int32(0)
    for member in range(count):
        place = jnp.where(index == member, table[member], place)
    return place


def ring_member(place, count):
    member = jnp.int32(0)
    for at, who in enumerate(ring_order(count)):
        member = jnp.where(place == at, who, member)
    return member


def ring_pairs(count, back=False):
    order = ring_order(count)
    pairs = [(order[i], order[(i + 1) % count]) for i in range(count)]
    return [(b, a) for a, b in pairs] if back else pairs


def doubling_sum(value, axis, wire):
    count = lax.axis_size(axis)
    if count & (count - 1):
        return lax.psum(value, axis)
    step = 1
    while step < count:
        pairs = [(i, i ^ step) for i in range(count)]
        sent = value.astype(wire)
        value = sent.astype(jnp.float32) + lax.ppermute(sent, axis, pairs).astype(jnp.float32)
        step *= 2
    return value


def rotation_tables(token_index_list):
    half_dim = HEAD_SIZE // 2
    frequency = 500000.0 ** (-(jnp.arange(half_dim, dtype=jnp.float32) * 2.0) / HEAD_SIZE)
    angles = token_index_list.astype(jnp.float32)[:, None] * frequency[None, :]
    return jnp.cos(angles)[:, None, :], jnp.sin(angles)[:, None, :]


def apply_rotation(values, tables):
    cosine, sine = tables
    half_dim = values.shape[-1] // 2
    first_half = values[..., :half_dim]
    second_half = values[..., half_dim:]
    return jnp.concatenate(
        [
            first_half * cosine - second_half * sine,
            second_half * cosine + first_half * sine,
        ],
        axis=-1,
    )


def token_positions(stored_block_order, first_row, row_count, half_rows):
    flat_index = first_row + jnp.arange(row_count, dtype=jnp.int32)
    block_index = flat_index // half_rows
    matches = (
        block_index[:, None] == jnp.arange(stored_block_order.shape[0], dtype=jnp.int32)[None, :]
    )
    stored_block = jnp.sum(jnp.where(matches, stored_block_order[None, :], 0), axis=1)
    return stored_block * half_rows + flat_index % half_rows


def shards(
    hidden,
    base_query_rows,
    base_key_rows,
    base_value_rows,
    stored_block_order,
    version,
    publisher,
    adapter_down_weight,
    adapter_up_query,
    adapter_up_key_value,
    output_down_weight,
    output_up_weight,
):
    rank = ADAPTER_RANK
    width = hidden.shape[1]
    source = publisher[0]
    chosen = lax.dynamic_index_in_dim(version, source, 0, keepdims=False)
    count = lax.axis_size("ctx")
    own_index = lax.axis_index("ctx")
    place = ring_place(own_index, count)
    behind = (place - ring_place(source, count)) % count
    is_source = behind == 0

    def pick(stored, first, rows):
        return lax.dynamic_slice(
            stored, (0, chosen, first, 0), (1, 1, rows, stored.shape[-1])
        ).reshape(rows, stored.shape[-1])

    pair_width = adapter_up_key_value.shape[-1]
    fold = width // pair_width
    pair_rows = 2 * rank // fold
    own_pair = lax.dynamic_index_in_dim(adapter_up_key_value[0], chosen, 0, keepdims=False)
    own_pair = own_pair.reshape(fold, pair_rows, pair_width).transpose(1, 0, 2)
    own_pair = own_pair.reshape(pair_rows, width)

    def pieces(stored, first, rows):
        return [pick(stored, first + i, CHUNK_ROWS) for i in range(0, rows, CHUNK_ROWS)]

    own = (
        pieces(adapter_down_weight, rank, 2 * rank)
        + pieces(adapter_down_weight, 0, rank)
        + [jnp.pad(own_pair, ((0, CHUNK_ROWS - pair_rows), (0, 0)))]
        + pieces(adapter_up_query, 0, rank)
        + pieces(output_down_weight, 0, rank)
        + pieces(output_up_weight, 0, rank)
    )
    per = rank // CHUNK_ROWS

    pairs = ring_pairs(count)
    arrived, sent = [], []
    for turn in range(len(own) + LAG * (count - 2)):
        if turn < LAG:
            moving = own[turn]
        else:
            moving = after(arrived[turn - LAG], sent[-1])
            if turn < len(own):
                moving = jnp.where(is_source, own[turn], moving)
        sent.append(moving)
        arrived.append(lax.ppermute(moving, "ctx", pairs))

    def chunk(k):
        return lax.select_n(
            behind, own[k], *[arrived[k + LAG * hop] for hop in range(count - 1)]
        )

    def chunks(first, number):
        return jnp.concatenate([chunk(first + i) for i in range(number)], axis=0)

    contract_last = (((1,), (1,)), ((), ()))
    local_rows = hidden.shape[0]
    half_rows = local_rows // 2
    local_heads = base_query_rows.shape[1] // HEAD_SIZE
    local_groups = base_key_rows.shape[1] // HEAD_SIZE
    group_size = local_heads // local_groups
    query_pos = token_positions(stored_block_order, own_index * local_rows, local_rows, half_rows)
    tables = rotation_tables(query_pos)

    part = lax.dot_general(
        hidden, chunks(0, 2 * per), contract_last, preferred_element_type=jnp.float32
    )
    pair_low = doubling_sum(part, "tp", jnp.float32).astype(jnp.bfloat16)
    part = lax.dot_general(
        hidden, chunks(2 * per, per), contract_last, preferred_element_type=jnp.float32
    )
    query_low = doubling_sum(part, "tp", jnp.float32).astype(jnp.bfloat16)

    up_pair = chunk(3 * per)[:pair_rows].reshape(pair_rows, fold, pair_width).transpose(1, 0, 2)
    up_pair = up_pair.reshape(2, rank, pair_width)
    keys = base_key_rows.astype(jnp.float32) + jnp.dot(
        pair_low[:, :rank], up_pair[0], preferred_element_type=jnp.float32
    )
    keys = apply_rotation(keys.reshape(local_rows, local_groups, HEAD_SIZE), tables)
    keys = keys.astype(jnp.bfloat16).reshape(local_rows, pair_width)
    values = base_value_rows.astype(jnp.float32) + jnp.dot(
        pair_low[:, rank:], up_pair[1], preferred_element_type=jnp.float32
    )
    values = values.astype(jnp.bfloat16)

    forward, backward = ring_pairs(count), ring_pairs(count, back=True)
    both = jnp.concatenate([keys, values], axis=1)
    blocks = {0: both}
    ahead, back = both, both
    for hop in range(1, (count - 1) // 2 + 1):
        ahead = lax.ppermute(ahead, "ctx", forward)
        back = lax.ppermute(back, "ctx", backward)
        blocks[-hop] = ahead
        blocks[hop] = back
    if count % 2 == 0:
        far_keys = lax.ppermute(ahead[:, :pair_width], "ctx", forward)
        far_values = lax.ppermute(back[:, pair_width:], "ctx", backward)
        blocks[count // 2] = jnp.concatenate([far_keys, far_values], axis=1)
    offsets = sorted(blocks)
    all_blocks = jnp.concatenate([blocks[o] for o in offsets], axis=0)
    key_pos = jnp.concatenate(
        [
            token_positions(
                stored_block_order,
                ring_member((place + o) % count, count) * local_rows,
                local_rows,
                half_rows,
            )
            for o in offsets
        ]
    )
    all_keys = all_blocks[:, :pair_width].reshape(-1, local_groups, HEAD_SIZE)
    all_values = all_blocks[:, pair_width:].reshape(-1, local_groups, HEAD_SIZE)

    queries = base_query_rows.astype(jnp.float32) + jnp.dot(
        query_low, chunks(3 * per + 1, per), preferred_element_type=jnp.float32
    )
    queries = apply_rotation(queries.reshape(local_rows, local_heads, HEAD_SIZE), tables)
    queries = queries.astype(jnp.bfloat16).reshape(
        local_rows, local_groups, group_size, HEAD_SIZE
    )

    scores = jnp.einsum(
        "tkgd,skd->kgts", queries, all_keys, preferred_element_type=jnp.float32
    ) * HEAD_SIZE ** (-0.5)
    visible = (key_pos[None, :] <= query_pos[:, None])[None, None]
    scores = jnp.where(visible, scores, NEG_BIG)
    largest = jnp.max(scores, axis=-1, keepdims=True)
    raw = jnp.where(visible, jnp.exp(scores - largest), 0.0)
    totals = jnp.sum(raw, axis=-1, keepdims=True)
    mixed = jnp.einsum(
        "kgts,skd->kgtd", raw.astype(jnp.bfloat16), all_values, preferred_element_type=jnp.float32
    )
    attended = (
        jnp.transpose(mixed / totals, (2, 0, 1, 3))
        .reshape(local_rows, local_heads * HEAD_SIZE)
        .astype(jnp.bfloat16)
    )
    out_part = lax.dot_general(
        attended, chunks(4 * per + 1, per), contract_last, preferred_element_type=jnp.float32
    )
    out_low = doubling_sum(out_part, "tp", jnp.float32).astype(jnp.bfloat16)
    adapted = jnp.dot(
        out_low, chunks(5 * per + 1, per), preferred_element_type=jnp.float32
    ).astype(jnp.bfloat16)
    return (attended, adapted)


def solution(mesh):
    placed = (
        P(("groups", "ctx"), "tp"),
        P(("groups", "ctx"), "tp"),
        P(("groups", "ctx"), "tp"),
        P(("groups", "ctx"), "tp"),
        P("groups"),
        P("groups"),
        P("groups"),
        P("ctx", None, None, "tp"),
        P("ctx", None, None, "tp"),
        P("ctx", None, None, None, "tp"),
        P("ctx", None, None, "tp"),
        P("ctx", None, None, "tp"),
    )
    return jax.shard_map(
        shards,
        mesh=mesh,
        in_specs=placed,
        out_specs=(P(("groups", "ctx"), "tp"), P(("groups", "ctx"), "tp")),
        check_vma=False,
    )
```

```python
import functools

import jax
import jax.numpy as jnp
from jax import lax
from jax.experimental import pallas as pl
from jax.experimental.pallas import tpu as pltpu
from jax.sharding import PartitionSpec as P


HEAD_SIZE = 128
ADAPTER_RANK = 64
NEG_BIG = -1e30
CHUNK_ROWS = 32
LAG = 2
PIECES = 2
KERNEL_VMEM = 8 << 20


def after(value, *earlier):
    return lax.optimization_barrier((value,) + earlier)[0]


def ring_order(count):
    return [0] + list(range(1, count, 2)) + list(range(2, count, 2))[::-1]


def ring_place(index, count):
    table = [0] * count
    for place, member in enumerate(ring_order(count)):
        table[member] = place
    place = jnp.int32(0)
    for member in range(count):
        place = jnp.where(index == member, table[member], place)
    return place


def ring_member(place, count):
    member = jnp.int32(0)
    for at, who in enumerate(ring_order(count)):
        member = jnp.where(place == at, who, member)
    return member


def ring_pairs(count, back=False):
    order = ring_order(count)
    pairs = [(order[i], order[(i + 1) % count]) for i in range(count)]
    return [(b, a) for a, b in pairs] if back else pairs


def doubling_sums(value, axis, wire):
    count = lax.axis_size(axis)
    if count & (count - 1):
        return [lax.psum(value, axis)]
    sums = []
    step = 1
    while step < count:
        pairs = [(i, i ^ step) for i in range(count)]
        sent = value.astype(wire)
        other = lax.ppermute(sent, axis, pairs)
        value = sent.astype(jnp.float32) + other.astype(jnp.float32)
        sums.append(value)
        step *= 2
    return sums


def rotation_tables(token_index_list):
    half_dim = HEAD_SIZE // 2
    frequency = 500000.0 ** (-(jnp.arange(half_dim, dtype=jnp.float32) * 2.0) / HEAD_SIZE)
    angles = token_index_list.astype(jnp.float32)[:, None] * frequency[None, :]
    cosine, sine = jnp.cos(angles), jnp.sin(angles)
    return jnp.concatenate([cosine, cosine, -sine, sine], axis=1)


def rotate(values, tables):
    swapped = pltpu.roll(values, HEAD_SIZE // 2, axis=1)
    return values * tables[:, :HEAD_SIZE] + swapped * tables[:, HEAD_SIZE:]


CONTRACT_LAST = (((1,), (1,)), ((), ()))
VMEM = pl.BlockSpec(memory_space=pltpu.VMEM)
SMEM = pl.BlockSpec(memory_space=pltpu.SMEM)


def chunk_call(kernel, behind, candidates, chunks, operands, out_shape):
    names = sorted(chunks)
    rows, width = chunks[names[0]].shape
    number = len(candidates[0])

    def body(behind_ref, *refs):
        chunk_refs = dict(zip(names, refs))
        weight_ref = refs[-1]
        for distance, held in enumerate(candidates):

            @pl.when(behind_ref[0] == distance)
            def _(held=held):
                for i, name in enumerate(held):
                    weight_ref[i * rows : (i + 1) * rows, :] = chunk_refs[name][...]

        kernel(weight_ref, *refs[len(names) : -1])

    return pl.pallas_call(
        body,
        out_shape=pltpu.VMEM(out_shape.shape, out_shape.dtype),
        in_specs=[SMEM] + [VMEM] * (len(names) + len(operands)),
        out_specs=VMEM,
        scratch_shapes=[pltpu.VMEM((number * rows, width), jnp.bfloat16)],
        compiler_params=pltpu.CompilerParams(vmem_limit_bytes=KERNEL_VMEM),
    )(
        behind,
        *[
            pltpu.with_memory_space_constraint(x, pltpu.VMEM)
            for x in [chunks[name] for name in names] + operands
        ],
    )


def low_kernel(weight_ref, *refs):
    out_ref = refs[-1]
    total, lane = None, 0
    for rows_ref in refs[:-1]:
        ends = lane + rows_ref.shape[1]
        part = lax.dot_general(
            rows_ref[...],
            weight_ref[:, lane:ends],
            CONTRACT_LAST,
            preferred_element_type=jnp.float32,
        )
        total = part if total is None else total + part
        lane = ends
    out_ref[...] = total


def up_kernel(weight_ref, low_ref, out_ref):
    out_ref[...] = jnp.dot(
        low_ref[...].astype(jnp.bfloat16), weight_ref[...], preferred_element_type=jnp.float32
    ).astype(out_ref.dtype)


def pair_kernel(weight_ref, low_ref, keys_ref, values_ref, tables_ref, out_ref):
    width = keys_ref.shape[1]
    rank = ADAPTER_RANK
    fold = weight_ref.shape[1] // width
    rows = 2 * rank // fold
    up = jnp.concatenate(
        [weight_ref[:rows, i * width : (i + 1) * width] for i in range(fold)], axis=0
    )
    low = low_ref[...].astype(jnp.bfloat16)
    keys = keys_ref[...].astype(jnp.float32) + jnp.dot(
        low[:, :rank], up[:rank], preferred_element_type=jnp.float32
    )
    values = values_ref[...].astype(jnp.float32) + jnp.dot(
        low[:, rank:], up[rank:], preferred_element_type=jnp.float32
    )
    for head in range(0, width, HEAD_SIZE):
        out_ref[:, head : head + HEAD_SIZE] = rotate(
            keys[:, head : head + HEAD_SIZE], tables_ref[...]
        ).astype(jnp.bfloat16)
    out_ref[:, width:] = values.astype(jnp.bfloat16)


def attend_kernel(
    first_head, group_size, block_count, weight_ref, low_ref, base_ref, tables_ref, query_pos_ref, key_pos_ref, *refs
):
    key_refs = refs[:block_count]
    value_refs = refs[block_count : 2 * block_count]
    out_ref = refs[-1]
    low = low_ref[...].astype(jnp.bfloat16)
    visible = key_pos_ref[...] <= query_pos_ref[...]
    group = None
    for lane in range(0, out_ref.shape[1], HEAD_SIZE):
        head = first_head + lane // HEAD_SIZE
        if head // group_size != group:
            group = head // group_size
            lanes = slice(group * HEAD_SIZE, (group + 1) * HEAD_SIZE)
            keys = jnp.concatenate([ref[:, lanes] for ref in key_refs], axis=0)
            values = jnp.concatenate([ref[:, lanes] for ref in value_refs], axis=0)
        at = slice(head * HEAD_SIZE, (head + 1) * HEAD_SIZE)
        queries = base_ref[:, at].astype(jnp.float32) + jnp.dot(
            low, weight_ref[:, at], preferred_element_type=jnp.float32
        )
        queries = rotate(queries, tables_ref[...]).astype(jnp.bfloat16)
        scores = lax.dot_general(
            queries, keys, CONTRACT_LAST, preferred_element_type=jnp.float32
        ) * HEAD_SIZE ** (-0.5)
        scores = jnp.where(visible, scores, NEG_BIG)
        raw = jnp.exp(scores - jnp.max(scores, axis=1, keepdims=True))
        totals = jnp.sum(raw, axis=1, keepdims=True)
        mixed = jnp.dot(raw.astype(jnp.bfloat16), values, preferred_element_type=jnp.float32)
        out_ref[:, lane : lane + HEAD_SIZE] = (mixed / totals).astype(jnp.bfloat16)


def token_positions(stored_block_order, first_row, row_count, half_rows):
    flat_index = first_row + jnp.arange(row_count, dtype=jnp.int32)
    block_index = flat_index // half_rows
    matches = (
        block_index[:, None] == jnp.arange(stored_block_order.shape[0], dtype=jnp.int32)[None, :]
    )
    stored_block = jnp.sum(jnp.where(matches, stored_block_order[None, :], 0), axis=1)
    return stored_block * half_rows + flat_index % half_rows


def shards(
    hidden,
    base_query_rows,
    base_key_rows,
    base_value_rows,
    stored_block_order,
    version,
    publisher,
    adapter_down_weight,
    adapter_up_query,
    adapter_up_key_value,
    output_down_weight,
    output_up_weight,
):
    rank = ADAPTER_RANK
    width = hidden.shape[1]
    source = publisher[0]
    slots = jnp.arange(version.shape[0], dtype=jnp.int32)
    chosen = jnp.sum(jnp.where(slots == source, version, 0))
    count = lax.axis_size("ctx")
    own_index = lax.axis_index("ctx")
    place = ring_place(own_index, count)
    behind = (place - ring_place(source, count)) % count
    is_source = behind == 0

    def pick(stored, first, rows):
        return lax.dynamic_slice(
            stored, (0, chosen, first, 0), (1, 1, rows, stored.shape[-1])
        ).reshape(rows, stored.shape[-1])

    pair_width = adapter_up_key_value.shape[-1]
    fold = width // pair_width
    pair_rows = 2 * rank // fold
    own_pair = lax.dynamic_index_in_dim(adapter_up_key_value[0], chosen, 0, keepdims=False)
    own_pair = own_pair.reshape(fold, pair_rows, pair_width).transpose(1, 0, 2)
    own_pair = own_pair.reshape(pair_rows, width)

    def pieces(stored, first, rows):
        return [pick(stored, first + i, CHUNK_ROWS) for i in range(0, rows, CHUNK_ROWS)]

    own = (
        pieces(adapter_down_weight, rank, 2 * rank)
        + pieces(adapter_down_weight, 0, rank)
        + [jnp.pad(own_pair, ((0, CHUNK_ROWS - pair_rows), (0, 0)))]
        + pieces(adapter_up_query, 0, rank)
        + pieces(output_down_weight, 0, rank)
        + pieces(output_up_weight, 0, rank)
    )
    per = rank // CHUNK_ROWS

    pairs = ring_pairs(count)
    arrived, sent = [], []
    own[LAG:] = lax.optimization_barrier(own[LAG:])

    def stream_to(last):
        for turn in range(len(sent), last):
            if turn < LAG:
                moving = own[turn]
            else:
                moving = after(arrived[turn - LAG], sent[-1])
                if turn < len(own):
                    moving = jnp.where(is_source, own[turn], moving)
            sent.append(moving)
            arrived.append(lax.ppermute(moving, "ctx", pairs))

    drain = LAG * (count - 2)

    distance = jnp.full((1,), behind, jnp.int32)

    def on_chunks(kernel, first, number, operands, shape, dtype):
        chunks = {("own", first + i): own[first + i] for i in range(number)}
        candidates = [[("own", first + i) for i in range(number)]]
        for hop in range(count - 1):
            turns = [first + i + LAG * hop for i in range(number)]
            candidates.append([("ring", turn) for turn in turns])
            chunks.update({("ring", turn): arrived[turn] for turn in turns})
        return chunk_call(
            kernel, distance, candidates, chunks, operands, jax.ShapeDtypeStruct(shape, dtype)
        )

    local_rows = hidden.shape[0]
    half_rows = local_rows // 2
    query_pos = token_positions(stored_block_order, own_index * local_rows, local_rows, half_rows)
    tables = rotation_tables(query_pos)

    stream_to(len(own) + drain)
    part = on_chunks(low_kernel, 0, 2 * per, [hidden], (local_rows, 2 * rank), jnp.float32)
    pair_sums = doubling_sums(part, "tp", jnp.float32)
    part = on_chunks(low_kernel, 2 * per, per, [hidden], (local_rows, rank), jnp.float32)
    query_sums = doubling_sums(part, "tp", jnp.float32)
    both = on_chunks(
        pair_kernel,
        3 * per,
        1,
        [pair_sums[-1], base_key_rows, base_value_rows, tables],
        (local_rows, 2 * pair_width),
        jnp.bfloat16,
    )

    forward, backward = ring_pairs(count), ring_pairs(count, back=True)
    key_blocks, value_blocks = {0: both[:, :pair_width]}, {0: both[:, pair_width:]}
    ahead, back = both, both
    for hop in range(1, (count - 1) // 2 + 1):
        ahead = lax.ppermute(ahead, "ctx", forward)
        back = lax.ppermute(back, "ctx", backward)
        for offset, block in ((-hop, ahead), (hop, back)):
            key_blocks[offset] = block[:, :pair_width]
            value_blocks[offset] = block[:, pair_width:]
    if count % 2 == 0:
        far = lax.ppermute(ahead[:, :pair_width], "ctx", forward)
        key_blocks[count // 2] = far
        far = lax.ppermute(back[:, pair_width:], "ctx", backward)
        value_blocks[count // 2] = far
    offsets = sorted(key_blocks)
    key_pos = jnp.concatenate(
        [
            token_positions(
                stored_block_order,
                ring_member((place + o) % count, count) * local_rows,
                local_rows,
                half_rows,
            )
            for o in offsets
        ]
    )
    local_heads = base_query_rows.shape[1] // HEAD_SIZE
    group_size = local_heads // (pair_width // HEAD_SIZE)
    piece_heads = local_heads // PIECES
    pieces_out = [
        on_chunks(
            functools.partial(attend_kernel, piece * piece_heads, group_size, len(offsets)),
            3 * per + 1,
            per,
            [query_sums[-1], base_query_rows, tables, query_pos[:, None], key_pos[None, :]]
            + [key_blocks[o] for o in offsets]
            + [value_blocks[o] for o in offsets],
            (local_rows, piece_heads * HEAD_SIZE),
            jnp.bfloat16,
        )
        for piece in range(PIECES)
    ]
    attended = jnp.concatenate(pieces_out, axis=1)
    late = 4 * per + 1
    part = on_chunks(low_kernel, late, per, pieces_out, (local_rows, rank), jnp.float32)
    out_low = doubling_sums(part, "tp", jnp.float32)[-1]
    adapted = on_chunks(up_kernel, late + per, per, [out_low], attended.shape, jnp.bfloat16)
    return (attended, adapted)


def solution(mesh):
    placed = (
        P(("groups", "ctx"), "tp"),
        P(("groups", "ctx"), "tp"),
        P(("groups", "ctx"), "tp"),
        P(("groups", "ctx"), "tp"),
        P("groups"),
        P("groups"),
        P("groups"),
        P("ctx", None, None, "tp"),
        P("ctx", None, None, "tp"),
        P("ctx", None, None, None, "tp"),
        P("ctx", None, None, "tp"),
        P("ctx", None, None, "tp"),
    )
    return jax.shard_map(
        shards,
        mesh=mesh,
        in_specs=placed,
        out_specs=(P(("groups", "ctx"), "tp"), P(("groups", "ctx"), "tp")),
        check_vma=False,
    )
```

```python
import functools
import math

import jax
import jax.numpy as jnp
from jax import lax
from jax.experimental import pallas as pl
from jax.experimental.pallas import tpu as pltpu
from jax.sharding import PartitionSpec as P


HEAD_SIZE = 128
ADAPTER_RANK = 64
NEG_BIG = -1e30
EXPONENT_SCALE = HEAD_SIZE ** (-0.5) * math.log2(math.e)
CHUNK_ROWS = 16
LAG = 4
PIECES = 4
KERNEL_VMEM = 8 << 20


def after(value, *earlier):
    return lax.optimization_barrier((value,) + earlier)[0]


def ring_order(count):
    return [0] + list(range(1, count, 2)) + list(range(2, count, 2))[::-1]


def ring_place(index, count):
    table = [0] * count
    for place, member in enumerate(ring_order(count)):
        table[member] = place
    place = jnp.int32(0)
    for member in range(count):
        place = jnp.where(index == member, table[member], place)
    return place


def ring_member(place, count):
    member = jnp.int32(0)
    for at, who in enumerate(ring_order(count)):
        member = jnp.where(place == at, who, member)
    return member


def ring_pairs(count, back=False):
    order = ring_order(count)
    pairs = [(order[i], order[(i + 1) % count]) for i in range(count)]
    return [(b, a) for a, b in pairs] if back else pairs


def doubling_sums(value, axis, wire):
    count = lax.axis_size(axis)
    if count & (count - 1):
        return [lax.psum(value, axis)]
    sums = []
    step = 1
    while step < count:
        pairs = [(i, i ^ step) for i in range(count)]
        sent = value.astype(wire)
        other = lax.ppermute(sent, axis, pairs)
        value = sent.astype(jnp.float32) + other.astype(jnp.float32)
        sums.append(value)
        step *= 2
    return sums


def rotation_tables(token_index_list):
    half_dim = HEAD_SIZE // 2
    frequency = 500000.0 ** (-(jnp.arange(half_dim, dtype=jnp.float32) * 2.0) / HEAD_SIZE)
    angles = token_index_list.astype(jnp.float32)[:, None] * frequency[None, :]
    cosine, sine = jnp.cos(angles), jnp.sin(angles)
    return jnp.concatenate([cosine, cosine, -sine, sine], axis=1)


def rotate(values, tables):
    swapped = pltpu.roll(values, HEAD_SIZE // 2, axis=1)
    return values * tables[:, :HEAD_SIZE] + swapped * tables[:, HEAD_SIZE:]


CONTRACT_LAST = (((1,), (1,)), ((), ()))
VMEM = pl.BlockSpec(memory_space=pltpu.VMEM)
SMEM = pl.BlockSpec(memory_space=pltpu.SMEM)


def chunk_call(kernel, behind, candidates, chunks, operands, out_shape):
    names = sorted(chunks)
    rows, width = CHUNK_ROWS, chunks[names[0]].shape[1]
    number = len(candidates[0])

    def body(behind_ref, *refs):
        chunk_refs = dict(zip(names, refs))
        weight_ref = refs[-1]
        for distance, held in enumerate(candidates):

            @pl.when(behind_ref[0] == distance)
            def _(held=held):
                for i, (name, row) in enumerate(held):
                    weight_ref[i * rows : (i + 1) * rows, :] = chunk_refs[name][row : row + rows]

        kernel(weight_ref, *refs[len(names) : -1])

    return pl.pallas_call(
        body,
        out_shape=pltpu.VMEM(out_shape.shape, out_shape.dtype),
        in_specs=[SMEM] + [VMEM] * (len(names) + len(operands)),
        out_specs=VMEM,
        scratch_shapes=[pltpu.VMEM((number * rows, width), jnp.bfloat16)],
        compiler_params=pltpu.CompilerParams(vmem_limit_bytes=KERNEL_VMEM),
    )(
        behind,
        *[
            pltpu.with_memory_space_constraint(x, pltpu.VMEM)
            for x in [chunks[name] for name in names] + operands
        ],
    )


def own_chunks(chunk_range, publisher, version, down, up_query, up_pair, out_down, out_up):
    rank = ADAPTER_RANK
    width = down.shape[-1]
    pair_width = up_pair.shape[-1]
    fold = width // pair_width
    pair_rows = 2 * rank // fold
    plan = [(0, rank + first) for first in range(0, 2 * rank, CHUNK_ROWS)] + [(2, 0)]
    plan += [(0, first) for first in range(0, rank, CHUNK_ROWS)]
    for weight in (1, 3, 4):
        plan += [(weight, first) for first in range(0, rank, CHUNK_ROWS)]
    plan = plan[chunk_range]

    def body(publisher_ref, version_ref, *refs):
        weights, outs, sem = refs[:5], refs[5:-1], refs[-1]
        chosen = version_ref[publisher_ref[0]]
        copies = []
        for (which, first), out in zip(plan, outs):
            if which != 2:
                rows = weights[which].at[0, chosen, pl.ds(first, CHUNK_ROWS)]
                copies.append((rows, out))
                continue
            for i in range(fold):
                half, row = divmod(i * pair_rows, rank)
                rows = weights[which].at[0, chosen, half, pl.ds(row, pair_rows)]
                lanes = pl.ds(i * pair_width, pair_width)
                copies.append((rows, out.at[pl.ds(0, pair_rows), lanes]))
        copies = [
            pltpu.make_async_copy(rows, out, sem.at[i]) for i, (rows, out) in enumerate(copies)
        ]
        for copy in copies:
            copy.start()
        for copy in copies:
            copy.wait()

    in_place = pl.BlockSpec(memory_space=pltpu.HBM)
    return pl.pallas_call(
        body,
        out_shape=[pltpu.VMEM((CHUNK_ROWS, width), jnp.bfloat16)] * len(plan),
        in_specs=[SMEM, SMEM] + [in_place] * 5,
        out_specs=[VMEM] * len(plan),
        scratch_shapes=[pltpu.SemaphoreType.DMA((len(plan) + fold - 1,))],
        compiler_params=pltpu.CompilerParams(vmem_limit_bytes=KERNEL_VMEM),
    )(
        publisher,
        version,
        *[
            pltpu.with_memory_space_constraint(x, pltpu.HBM)
            for x in (down, up_query, up_pair, out_down, out_up)
        ],
    )


def low_kernel(weight_ref, *refs):
    out_ref = refs[-1]
    total, lane = None, 0
    for rows_ref in refs[:-1]:
        ends = lane + rows_ref.shape[1]
        part = lax.dot_general(
            rows_ref[...],
            weight_ref[:, lane:ends],
            CONTRACT_LAST,
            preferred_element_type=jnp.float32,
        )
        total = part if total is None else total + part
        lane = ends
    out_ref[...] = total


def up_kernel(weight_ref, low_ref, out_ref):
    out_ref[...] = jnp.dot(
        low_ref[...].astype(jnp.bfloat16), weight_ref[...], preferred_element_type=jnp.float32
    ).astype(out_ref.dtype)


def pair_kernel(weight_ref, low_ref, keys_ref, values_ref, tables_ref, out_ref):
    width = keys_ref.shape[1]
    rank = ADAPTER_RANK
    fold = weight_ref.shape[1] // width
    rows = 2 * rank // fold
    up = jnp.concatenate(
        [weight_ref[:rows, i * width : (i + 1) * width] for i in range(fold)], axis=0
    )
    low = low_ref[...].astype(jnp.bfloat16)
    keys = keys_ref[...].astype(jnp.float32) + jnp.dot(
        low[:, :rank], up[:rank], preferred_element_type=jnp.float32
    )
    values = values_ref[...].astype(jnp.float32) + jnp.dot(
        low[:, rank:], up[rank:], preferred_element_type=jnp.float32
    )
    for head in range(0, width, HEAD_SIZE):
        out_ref[:, head : head + HEAD_SIZE] = rotate(
            keys[:, head : head + HEAD_SIZE], tables_ref[...]
        ).astype(jnp.bfloat16)
    out_ref[:, width:] = values.astype(jnp.bfloat16)


def attend_kernel(
    first_head, group_size, block_count, weight_ref, low_ref, base_ref, tables_ref, hidden_ref, *refs
):
    key_refs = refs[:block_count]
    value_refs = refs[block_count : 2 * block_count]
    out_ref = refs[-1]
    low = low_ref[...].astype(jnp.bfloat16)
    group = None
    for lane in range(0, out_ref.shape[1], HEAD_SIZE):
        head = first_head + lane // HEAD_SIZE
        if head // group_size != group:
            group = head // group_size
            lanes = slice(group * HEAD_SIZE, (group + 1) * HEAD_SIZE)
            keys = jnp.concatenate([ref[:, lanes] for ref in key_refs], axis=0)
            values = jnp.concatenate([ref[:, lanes] for ref in value_refs], axis=0)
        at = slice(head * HEAD_SIZE, (head + 1) * HEAD_SIZE)
        queries = base_ref[:, at].astype(jnp.float32) + jnp.dot(
            low, weight_ref[:, at], preferred_element_type=jnp.float32
        )
        queries = rotate(queries, tables_ref[...]).astype(jnp.bfloat16)
        scores = lax.dot_general(
            queries, keys, CONTRACT_LAST, preferred_element_type=jnp.float32
        )
        scores = scores + hidden_ref[...]
        raw = jnp.exp2((scores - jnp.max(scores, axis=1, keepdims=True)) * EXPONENT_SCALE)
        totals = jnp.sum(raw, axis=1, keepdims=True)
        mixed = jnp.dot(raw.astype(jnp.bfloat16), values, preferred_element_type=jnp.float32)
        out_ref[:, lane : lane + HEAD_SIZE] = (mixed / totals).astype(jnp.bfloat16)


def token_positions(stored_block_order, first_row, row_count, half_rows):
    flat_index = first_row + jnp.arange(row_count, dtype=jnp.int32)
    block_index = flat_index // half_rows
    matches = (
        block_index[:, None] == jnp.arange(stored_block_order.shape[0], dtype=jnp.int32)[None, :]
    )
    stored_block = jnp.sum(jnp.where(matches, stored_block_order[None, :], 0), axis=1)
    return stored_block * half_rows + flat_index % half_rows


def shards(
    hidden,
    base_query_rows,
    base_key_rows,
    base_value_rows,
    stored_block_order,
    version,
    publisher,
    adapter_down_weight,
    adapter_up_query,
    adapter_up_key_value,
    output_down_weight,
    output_up_weight,
):
    rank = ADAPTER_RANK
    count = lax.axis_size("ctx")
    own_index = lax.axis_index("ctx")
    place = ring_place(own_index, count)
    pair_width = adapter_up_key_value.shape[-1]
    weights = (
        adapter_down_weight,
        adapter_up_query,
        adapter_up_key_value,
        output_down_weight,
        output_up_weight,
    )
    own = []
    for chunk_range in (slice(0, LAG), slice(LAG, None)):
        own += own_chunks(chunk_range, publisher, version, *weights)
    per = rank // CHUNK_ROWS

    pairs = ring_pairs(count)
    arrived, sent = [], []
    for turn in range(LAG):
        sent.append(own[turn])
        arrived.append(lax.ppermute(own[turn], "ctx", pairs))
    source = after(publisher, *sent)[0]
    behind = (place - ring_place(source, count)) % count
    is_source = behind == 0
    for turn in range(LAG, len(own)):
        moving = after(arrived[turn - LAG], sent[-1])
        moving = jnp.where(is_source, own[turn], moving)
        sent.append(moving)
        arrived.append(lax.ppermute(moving, "ctx", pairs))
    late = []
    for _ in range(count - 2):
        moving = late[-1] if late else jnp.concatenate(arrived[-LAG:], axis=0)
        late.append(lax.ppermute(moving, "ctx", pairs))
    stored_block_order = after(stored_block_order, sent[3 * LAG])

    distance = jnp.full((1,), behind, jnp.int32)

    def on_chunks(kernel, first, number, operands, shape, dtype):
        chunks, candidates = {}, []
        for hop in range(-1, count - 1):
            held = []
            for k in range(first, first + number):
                turn = k + LAG * hop
                if hop < 0:
                    key, row, array = ("own", k), 0, own[k]
                elif turn < len(own):
                    key, row, array = ("ring", turn), 0, arrived[turn]
                else:
                    group, row = divmod(turn - len(own), LAG)
                    key, row, array = ("late", group), row * CHUNK_ROWS, late[group]
                chunks[key] = array
                held.append((key, row))
            candidates.append(held)
        return chunk_call(
            kernel, distance, candidates, chunks, operands, jax.ShapeDtypeStruct(shape, dtype)
        )

    local_rows = hidden.shape[0]
    half_rows = local_rows // 2
    query_pos = token_positions(stored_block_order, own_index * local_rows, local_rows, half_rows)
    tables = rotation_tables(query_pos)

    part = on_chunks(low_kernel, 0, 2 * per, [hidden], (local_rows, 2 * rank), jnp.float32)
    pair_sums = doubling_sums(part, "tp", jnp.float32)
    part = on_chunks(low_kernel, 2 * per + 1, per, [hidden], (local_rows, rank), jnp.float32)
    query_sums = doubling_sums(part, "tp", jnp.float32)
    both = on_chunks(
        pair_kernel,
        2 * per,
        1,
        [pair_sums[-1], base_key_rows, base_value_rows, tables],
        (local_rows, 2 * pair_width),
        jnp.bfloat16,
    )

    forward, backward = ring_pairs(count), ring_pairs(count, back=True)
    key_blocks, value_blocks = {0: both[:, :pair_width]}, {0: both[:, pair_width:]}
    ahead, back = both, both
    for hop in range(1, (count - 1) // 2 + 1):
        ahead = lax.ppermute(ahead, "ctx", forward)
        back = lax.ppermute(back, "ctx", backward)
        for offset, block in ((-hop, ahead), (hop, back)):
            key_blocks[offset] = block[:, :pair_width]
            value_blocks[offset] = block[:, pair_width:]
    if count % 2 == 0:
        far = lax.ppermute(ahead[:, :pair_width], "ctx", forward)
        key_blocks[count // 2] = far
        far = lax.ppermute(back[:, pair_width:], "ctx", backward)
        value_blocks[count // 2] = far
    offsets = sorted(key_blocks)
    key_pos = jnp.concatenate(
        [
            token_positions(
                stored_block_order,
                ring_member((place + o) % count, count) * local_rows,
                local_rows,
                half_rows,
            )
            for o in offsets
        ]
    )
    hide = jnp.where(key_pos[None, :] <= query_pos[:, None], 0.0, NEG_BIG)
    local_heads = base_query_rows.shape[1] // HEAD_SIZE
    group_size = local_heads // (pair_width // HEAD_SIZE)
    piece_heads = local_heads // PIECES
    pieces_out = [
        on_chunks(
            functools.partial(attend_kernel, piece * piece_heads, group_size, len(offsets)),
            3 * per + 1,
            per,
            [query_sums[-1], base_query_rows, tables, hide]
            + [key_blocks[o] for o in offsets]
            + [value_blocks[o] for o in offsets],
            (local_rows, piece_heads * HEAD_SIZE),
            jnp.bfloat16,
        )
        for piece in range(PIECES)
    ]
    attended = jnp.concatenate(pieces_out, axis=1)
    part = on_chunks(low_kernel, 4 * per + 1, per, pieces_out, (local_rows, rank), jnp.float32)
    out_low = doubling_sums(part, "tp", jnp.float32)[-1]
    adapted = on_chunks(up_kernel, 5 * per + 1, per, [out_low], attended.shape, jnp.bfloat16)
    return (attended, adapted)


def solution(mesh):
    placed = (
        P(("groups", "ctx"), "tp"),
        P(("groups", "ctx"), "tp"),
        P(("groups", "ctx"), "tp"),
        P(("groups", "ctx"), "tp"),
        P("groups"),
        P("groups"),
        P("groups"),
        P("ctx", None, None, "tp"),
        P("ctx", None, None, "tp"),
        P("ctx", None, None, None, "tp"),
        P("ctx", None, None, "tp"),
        P("ctx", None, None, "tp"),
    )
    return jax.shard_map(
        shards,
        mesh=mesh,
        in_specs=placed,
        out_specs=(P(("groups", "ctx"), "tp"), P(("groups", "ctx"), "tp")),
        check_vma=False,
    )
```

```python
import functools
import math

import jax
import jax.numpy as jnp
from jax import lax
from jax.experimental import pallas as pl
from jax.experimental.pallas import tpu as pltpu
from jax.sharding import PartitionSpec as P


HEAD_SIZE = 128
ADAPTER_RANK = 64
NEG_BIG = -1e30
EXPONENT_SCALE = HEAD_SIZE ** (-0.5) * math.log2(math.e)
CHUNK_ROWS = 16
LAG = 4
PIECES = 1
JOINED = 2
KERNEL_VMEM = 8 << 20


def after(value, *earlier):
    return lax.optimization_barrier((value,) + earlier)[0]


def ring_order(count):
    return [0] + list(range(1, count, 2)) + list(range(2, count, 2))[::-1]


def ring_place(index, count):
    table = [0] * count
    for place, member in enumerate(ring_order(count)):
        table[member] = place
    place = jnp.int32(0)
    for member in range(count):
        place = jnp.where(index == member, table[member], place)
    return place


def ring_member(place, count):
    member = jnp.int32(0)
    for at, who in enumerate(ring_order(count)):
        member = jnp.where(place == at, who, member)
    return member


def ring_pairs(count, back=False):
    order = ring_order(count)
    pairs = [(order[i], order[(i + 1) % count]) for i in range(count)]
    return [(b, a) for a, b in pairs] if back else pairs


def doubling_sums(value, axis, wire):
    count = lax.axis_size(axis)
    if count & (count - 1):
        return [lax.psum(value, axis)]
    sums = []
    step = 1
    while step < count:
        pairs = [(i, i ^ step) for i in range(count)]
        sent = value.astype(wire)
        other = lax.ppermute(sent, axis, pairs)
        value = sent.astype(jnp.float32) + other.astype(jnp.float32)
        sums.append(value)
        step *= 2
    return sums


def rotation_tables(token_index_list):
    half_dim = HEAD_SIZE // 2
    frequency = 500000.0 ** (-(jnp.arange(half_dim, dtype=jnp.float32) * 2.0) / HEAD_SIZE)
    angles = token_index_list.astype(jnp.float32)[:, None] * frequency[None, :]
    cosine, sine = jnp.cos(angles), jnp.sin(angles)
    return jnp.concatenate([cosine, cosine, -sine, sine], axis=1)


def rotate(values, tables):
    swapped = pltpu.roll(values, HEAD_SIZE // 2, axis=1)
    return values * tables[:, :HEAD_SIZE] + swapped * tables[:, HEAD_SIZE:]


CONTRACT_LAST = (((1,), (1,)), ((), ()))
CONTRACT_FIRST = (((0,), (0,)), ((), ()))
VMEM = pl.BlockSpec(memory_space=pltpu.VMEM)
SMEM = pl.BlockSpec(memory_space=pltpu.SMEM)


def chunk_call(kernel, behind, candidates, chunks, operands, out_shape):
    names = sorted(chunks)
    rows, width = CHUNK_ROWS, chunks[names[0]].shape[1]
    number = len(candidates[0])

    def body(behind_ref, *refs):
        chunk_refs = dict(zip(names, refs))
        weight_ref = refs[-1]
        for distance, held in enumerate(candidates):

            @pl.when(behind_ref[0] == distance)
            def _(held=held):
                for i, (name, row) in enumerate(held):
                    weight_ref[i * rows : (i + 1) * rows, :] = chunk_refs[name][row : row + rows]

        kernel(weight_ref, *refs[len(names) : -1])

    return pl.pallas_call(
        body,
        out_shape=pltpu.VMEM(out_shape.shape, out_shape.dtype),
        in_specs=[SMEM] + [VMEM] * (len(names) + len(operands)),
        out_specs=VMEM,
        scratch_shapes=[pltpu.VMEM((number * rows, width), jnp.bfloat16)],
        compiler_params=pltpu.CompilerParams(vmem_limit_bytes=KERNEL_VMEM),
    )(
        behind,
        *[
            pltpu.with_memory_space_constraint(x, pltpu.VMEM)
            for x in [chunks[name] for name in names] + operands
        ],
    )


def own_chunks(chunk_range, publisher, version, down, up_query, up_pair, out_down, out_up):
    rank = ADAPTER_RANK
    width = down.shape[-1]
    pair_width = up_pair.shape[-1]
    fold = width // pair_width
    pair_rows = 2 * rank // fold
    plan = [(0, rank + first) for first in range(0, 2 * rank, CHUNK_ROWS)] + [(2, 0)]
    plan += [(0, first) for first in range(0, rank, CHUNK_ROWS)]
    for weight in (1, 3, 4):
        plan += [(weight, first) for first in range(0, rank, CHUNK_ROWS)]
    plan = plan[chunk_range]

    def body(publisher_ref, version_ref, *refs):
        weights, outs, sem = refs[:5], refs[5:-1], refs[-1]
        chosen = version_ref[publisher_ref[0]]
        copies = []
        for (which, first), out in zip(plan, outs):
            if which != 2:
                rows = weights[which].at[0, chosen, pl.ds(first, CHUNK_ROWS)]
                copies.append((rows, out))
                continue
            for i in range(fold):
                half, row = divmod(i * pair_rows, rank)
                rows = weights[which].at[0, chosen, half, pl.ds(row, pair_rows)]
                lanes = pl.ds(i * pair_width, pair_width)
                copies.append((rows, out.at[pl.ds(0, pair_rows), lanes]))
        copies = [
            pltpu.make_async_copy(rows, out, sem.at[i]) for i, (rows, out) in enumerate(copies)
        ]
        for copy in copies:
            copy.start()
        for copy in copies:
            copy.wait()

    in_place = pl.BlockSpec(memory_space=pltpu.HBM)
    return pl.pallas_call(
        body,
        out_shape=[pltpu.VMEM((CHUNK_ROWS, width), jnp.bfloat16)] * len(plan),
        in_specs=[SMEM, SMEM] + [in_place] * 5,
        out_specs=[VMEM] * len(plan),
        scratch_shapes=[pltpu.SemaphoreType.DMA((len(plan) + fold - 1,))],
        compiler_params=pltpu.CompilerParams(vmem_limit_bytes=KERNEL_VMEM),
    )(
        publisher,
        version,
        *[
            pltpu.with_memory_space_constraint(x, pltpu.HBM)
            for x in (down, up_query, up_pair, out_down, out_up)
        ],
    )


def low_kernel(weight_ref, *refs):
    out_ref = refs[-1]
    total, lane = None, 0
    for rows_ref in refs[:-1]:
        ends = lane + rows_ref.shape[1]
        part = lax.dot_general(
            rows_ref[...],
            weight_ref[:, lane:ends],
            CONTRACT_LAST,
            preferred_element_type=jnp.float32,
        )
        total = part if total is None else total + part
        lane = ends
    out_ref[...] = total


def up_kernel(weight_ref, low_ref, out_ref):
    out_ref[...] = jnp.dot(
        low_ref[...].astype(jnp.bfloat16), weight_ref[...], preferred_element_type=jnp.float32
    ).astype(out_ref.dtype)


def pair_kernel(weight_ref, low_ref, keys_ref, values_ref, tables_ref, out_ref):
    width = keys_ref.shape[1]
    rank = ADAPTER_RANK
    fold = weight_ref.shape[1] // width
    rows = 2 * rank // fold
    up = jnp.concatenate(
        [weight_ref[:rows, i * width : (i + 1) * width] for i in range(fold)], axis=0
    )
    low = low_ref[...].astype(jnp.bfloat16)
    keys = keys_ref[...].astype(jnp.float32) + jnp.dot(
        low[:, :rank], up[:rank], preferred_element_type=jnp.float32
    )
    values = values_ref[...].astype(jnp.float32) + jnp.dot(
        low[:, rank:], up[rank:], preferred_element_type=jnp.float32
    )
    for head in range(0, width, HEAD_SIZE):
        out_ref[:, head : head + HEAD_SIZE] = rotate(
            keys[:, head : head + HEAD_SIZE], tables_ref[...]
        ).astype(jnp.bfloat16)
    out_ref[:, width:] = values.astype(jnp.bfloat16)


def attend_kernel(
    first_head, group_size, block_count, weight_ref, low_ref, base_ref, tables_ref, hidden_ref, *refs
):
    key_refs = refs[:block_count]
    value_refs = refs[block_count : 2 * block_count]
    out_ref = refs[-1]
    low = low_ref[...].astype(jnp.bfloat16)
    first = first_head * HEAD_SIZE
    queries = base_ref[:, first : first + out_ref.shape[1]].astype(jnp.float32) + jnp.dot(
        low, weight_ref[:, first : first + out_ref.shape[1]], preferred_element_type=jnp.float32
    )
    group = None
    for lane in range(0, out_ref.shape[1], HEAD_SIZE):
        head = first_head + lane // HEAD_SIZE
        if head // group_size != group:
            group = head // group_size
            lanes = slice(group * HEAD_SIZE, (group + 1) * HEAD_SIZE)
            keys = jnp.concatenate([ref[:, lanes] for ref in key_refs], axis=0)
            values = jnp.concatenate([ref[:, lanes] for ref in value_refs], axis=0)
        turned = rotate(queries[:, lane : lane + HEAD_SIZE], tables_ref[...]).astype(jnp.bfloat16)
        scores = lax.dot_general(
            keys, turned, CONTRACT_LAST, preferred_element_type=jnp.float32
        )
        scores = scores + hidden_ref[...]
        raw = jnp.exp2((scores - jnp.max(scores, axis=0, keepdims=True)) * EXPONENT_SCALE)
        totals = jnp.sum(raw, axis=0, keepdims=True)
        mixed = lax.dot_general(
            values, raw.astype(jnp.bfloat16), CONTRACT_FIRST, preferred_element_type=jnp.float32
        )
        out_ref[:, lane : lane + HEAD_SIZE] = (mixed / totals).T.astype(jnp.bfloat16)


def token_positions(stored_block_order, first_row, row_count, half_rows):
    flat_index = first_row + jnp.arange(row_count, dtype=jnp.int32)
    block_index = flat_index // half_rows
    matches = (
        block_index[:, None] == jnp.arange(stored_block_order.shape[0], dtype=jnp.int32)[None, :]
    )
    stored_block = jnp.sum(jnp.where(matches, stored_block_order[None, :], 0), axis=1)
    return stored_block * half_rows + flat_index % half_rows


def shards(
    hidden,
    base_query_rows,
    base_key_rows,
    base_value_rows,
    stored_block_order,
    version,
    publisher,
    adapter_down_weight,
    adapter_up_query,
    adapter_up_key_value,
    output_down_weight,
    output_up_weight,
):
    rank = ADAPTER_RANK
    count = lax.axis_size("ctx")
    own_index = lax.axis_index("ctx")
    place = ring_place(own_index, count)
    pair_width = adapter_up_key_value.shape[-1]
    weights = (
        adapter_down_weight,
        adapter_up_query,
        adapter_up_key_value,
        output_down_weight,
        output_up_weight,
    )
    own = []
    for chunk_range in (slice(0, LAG), slice(LAG, None)):
        own += own_chunks(chunk_range, publisher, version, *weights)
    per = rank // CHUNK_ROWS

    pairs = ring_pairs(count)
    arrived, sent = [], []
    for turn in range(LAG):
        sent.append(own[turn])
        arrived.append(lax.ppermute(own[turn], "ctx", pairs))
    source = after(publisher, *sent)[0]
    behind = (place - ring_place(source, count)) % count
    is_source = behind == 0
    for turn in range(LAG, len(own)):
        moving = after(arrived[turn - LAG], sent[-1])
        moving = jnp.where(is_source, own[turn], moving)
        sent.append(moving)
        arrived.append(lax.ppermute(moving, "ctx", pairs))
    late = []
    for turn in range(LAG * (count - 2) // JOINED):
        if turn < LAG // JOINED:
            first = len(own) - LAG + turn * JOINED
            moving = jnp.concatenate(arrived[first : first + JOINED], axis=0)
        else:
            moving = late[turn - LAG // JOINED]
        late.append(lax.ppermute(moving, "ctx", pairs))
    stored_block_order = after(stored_block_order, sent[3 * LAG])

    distance = jnp.full((1,), behind, jnp.int32)

    def on_chunks(kernel, first, number, operands, shape, dtype):
        chunks, candidates = {}, []
        for hop in range(-1, count - 1):
            held = []
            for k in range(first, first + number):
                turn = k + LAG * hop
                if hop < 0:
                    key, row, array = ("own", k), 0, own[k]
                elif turn < len(own):
                    key, row, array = ("ring", turn), 0, arrived[turn]
                else:
                    group, row = divmod(turn - len(own), JOINED)
                    key, row, array = ("late", group), row * CHUNK_ROWS, late[group]
                chunks[key] = array
                held.append((key, row))
            candidates.append(held)
        return chunk_call(
            kernel, distance, candidates, chunks, operands, jax.ShapeDtypeStruct(shape, dtype)
        )

    local_rows = hidden.shape[0]
    half_rows = local_rows // 2
    query_pos = token_positions(stored_block_order, own_index * local_rows, local_rows, half_rows)
    tables = rotation_tables(query_pos)

    part = on_chunks(low_kernel, 0, 2 * per, [hidden], (local_rows, 2 * rank), jnp.float32)
    pair_sums = doubling_sums(part, "tp", jnp.float32)
    part = on_chunks(low_kernel, 2 * per + 1, per, [hidden], (local_rows, rank), jnp.float32)
    query_sums = doubling_sums(part, "tp", jnp.float32)
    both = on_chunks(
        pair_kernel,
        2 * per,
        1,
        [pair_sums[-1], base_key_rows, base_value_rows, tables],
        (local_rows, 2 * pair_width),
        jnp.bfloat16,
    )

    forward, backward = ring_pairs(count), ring_pairs(count, back=True)
    key_blocks, value_blocks = {0: both[:, :pair_width]}, {0: both[:, pair_width:]}
    ahead, back = both, both
    for hop in range(1, (count - 1) // 2 + 1):
        ahead = lax.ppermute(ahead, "ctx", forward)
        back = lax.ppermute(back, "ctx", backward)
        for offset, block in ((-hop, ahead), (hop, back)):
            key_blocks[offset] = block[:, :pair_width]
            value_blocks[offset] = block[:, pair_width:]
    if count % 2 == 0:
        far = lax.ppermute(ahead[:, :pair_width], "ctx", forward)
        key_blocks[count // 2] = far
        far = lax.ppermute(back[:, pair_width:], "ctx", backward)
        value_blocks[count // 2] = far
    offsets = sorted(key_blocks)
    key_pos = jnp.concatenate(
        [
            token_positions(
                stored_block_order,
                ring_member((place + o) % count, count) * local_rows,
                local_rows,
                half_rows,
            )
            for o in offsets
        ]
    )
    hide = jnp.where(key_pos[:, None] <= query_pos[None, :], 0.0, NEG_BIG)
    local_heads = base_query_rows.shape[1] // HEAD_SIZE
    group_size = local_heads // (pair_width // HEAD_SIZE)
    piece_heads = local_heads // PIECES
    pieces_out = [
        on_chunks(
            functools.partial(attend_kernel, piece * piece_heads, group_size, len(offsets)),
            3 * per + 1,
            per,
            [query_sums[-1], base_query_rows, tables, hide]
            + [key_blocks[o] for o in offsets]
            + [value_blocks[o] for o in offsets],
            (local_rows, piece_heads * HEAD_SIZE),
            jnp.bfloat16,
        )
        for piece in range(PIECES)
    ]
    attended = jnp.concatenate(pieces_out, axis=1)
    part = on_chunks(low_kernel, 4 * per + 1, per, pieces_out, (local_rows, rank), jnp.float32)
    out_low = doubling_sums(part, "tp", jnp.float32)[-1]
    adapted = on_chunks(up_kernel, 5 * per + 1, per, [out_low], attended.shape, jnp.bfloat16)
    return (attended, adapted)


def solution(mesh):
    placed = (
        P(("groups", "ctx"), "tp"),
        P(("groups", "ctx"), "tp"),
        P(("groups", "ctx"), "tp"),
        P(("groups", "ctx"), "tp"),
        P("groups"),
        P("groups"),
        P("groups"),
        P("ctx", None, None, "tp"),
        P("ctx", None, None, "tp"),
        P("ctx", None, None, None, "tp"),
        P("ctx", None, None, "tp"),
        P("ctx", None, None, "tp"),
    )
    return jax.shard_map(
        shards,
        mesh=mesh,
        in_specs=placed,
        out_specs=(P(("groups", "ctx"), "tp"), P(("groups", "ctx"), "tp")),
        check_vma=False,
    )
```

```python
import functools
import math

import jax
import jax.numpy as jnp
from jax import lax
from jax.experimental import pallas as pl
from jax.experimental.pallas import tpu as pltpu
from jax.sharding import PartitionSpec as P


HEAD_SIZE = 128
ADAPTER_RANK = 64
NEG_BIG = -1e30
EXPONENT_SCALE = HEAD_SIZE ** (-0.5) * math.log2(math.e)
CHUNK_ROWS = 16
LAG = 4
JOINED = 2
KERNEL_VMEM = 8 << 20


def after(value, *earlier):
    return lax.optimization_barrier((value,) + earlier)[0]


def ring_order(count):
    return [0] + list(range(1, count, 2)) + list(range(2, count, 2))[::-1]


def ring_place(index, count):
    table = [0] * count
    for place, member in enumerate(ring_order(count)):
        table[member] = place
    place = jnp.int32(0)
    for member in range(count):
        place = jnp.where(index == member, table[member], place)
    return place


def ring_member(place, count):
    member = jnp.int32(0)
    for at, who in enumerate(ring_order(count)):
        member = jnp.where(place == at, who, member)
    return member


def ring_pairs(count, back=False):
    order = ring_order(count)
    pairs = [(order[i], order[(i + 1) % count]) for i in range(count)]
    return [(b, a) for a, b in pairs] if back else pairs


def doubling_sums(value, axis, wire):
    count = lax.axis_size(axis)
    if count & (count - 1):
        return [lax.psum(value, axis)]
    sums = []
    step = 1
    while step < count:
        pairs = [(i, i ^ step) for i in range(count)]
        sent = value.astype(wire)
        other = lax.ppermute(sent, axis, pairs)
        value = sent.astype(jnp.float32) + other.astype(jnp.float32)
        sums.append(value)
        step *= 2
    return sums


def rotation_tables(token_index_list):
    half_dim = HEAD_SIZE // 2
    frequency = 500000.0 ** (-(jnp.arange(half_dim, dtype=jnp.float32) * 2.0) / HEAD_SIZE)
    angles = token_index_list.astype(jnp.float32)[:, None] * frequency[None, :]
    cosine, sine = jnp.cos(angles), jnp.sin(angles)
    return jnp.concatenate([cosine, cosine, -sine, sine], axis=1)


def rotate(values, tables):
    swapped = pltpu.roll(values, HEAD_SIZE // 2, axis=1)
    return values * tables[:, :HEAD_SIZE] + swapped * tables[:, HEAD_SIZE:]


CONTRACT_LAST = (((1,), (1,)), ((), ()))
CONTRACT_FIRST = (((0,), (0,)), ((), ()))
VMEM = pl.BlockSpec(memory_space=pltpu.VMEM)
SMEM = pl.BlockSpec(memory_space=pltpu.SMEM)


def chunk_call(kernel, behind, candidates, chunks, operands, out_shape):
    names = sorted(chunks)
    rows, width = CHUNK_ROWS, chunks[names[0]].shape[1]
    number = len(candidates[0])

    def body(behind_ref, *refs):
        chunk_refs = dict(zip(names, refs))
        weight_ref = refs[-1]
        for distance, held in enumerate(candidates):

            @pl.when(behind_ref[0] == distance)
            def _(held=held):
                for i, (name, row) in enumerate(held):
                    weight_ref[i * rows : (i + 1) * rows, :] = chunk_refs[name][row : row + rows]

        kernel(weight_ref, *refs[len(names) : -1])

    return pl.pallas_call(
        body,
        out_shape=pltpu.VMEM(out_shape.shape, out_shape.dtype),
        in_specs=[SMEM] + [VMEM] * (len(names) + len(operands)),
        out_specs=VMEM,
        scratch_shapes=[pltpu.VMEM((number * rows, width), jnp.bfloat16)],
        compiler_params=pltpu.CompilerParams(vmem_limit_bytes=KERNEL_VMEM),
    )(
        behind,
        *[
            pltpu.with_memory_space_constraint(x, pltpu.VMEM)
            for x in [chunks[name] for name in names] + operands
        ],
    )


def own_chunks(chunk_range, publisher, version, down, up_query, up_pair, out_down, out_up):
    rank = ADAPTER_RANK
    width = down.shape[-1]
    pair_width = up_pair.shape[-1]
    fold = width // pair_width
    pair_rows = 2 * rank // fold
    plan = [(0, rank + first) for first in range(0, 2 * rank, CHUNK_ROWS)] + [(2, 0)]
    plan += [(0, first) for first in range(0, rank, CHUNK_ROWS)]
    for weight in (1, 3, 4):
        plan += [(weight, first) for first in range(0, rank, CHUNK_ROWS)]
    plan = plan[chunk_range]

    def body(publisher_ref, version_ref, *refs):
        weights, outs, sem = refs[:5], refs[5:-1], refs[-1]
        chosen = version_ref[publisher_ref[0]]
        copies = []
        for (which, first), out in zip(plan, outs):
            if which != 2:
                rows = weights[which].at[0, chosen, pl.ds(first, CHUNK_ROWS)]
                copies.append((rows, out))
                continue
            for i in range(fold):
                half, row = divmod(i * pair_rows, rank)
                rows = weights[which].at[0, chosen, half, pl.ds(row, pair_rows)]
                lanes = pl.ds(i * pair_width, pair_width)
                copies.append((rows, out.at[pl.ds(0, pair_rows), lanes]))
        copies = [
            pltpu.make_async_copy(rows, out, sem.at[i]) for i, (rows, out) in enumerate(copies)
        ]
        for copy in copies:
            copy.start()
        for copy in copies:
            copy.wait()

    in_place = pl.BlockSpec(memory_space=pltpu.HBM)
    return pl.pallas_call(
        body,
        out_shape=[pltpu.VMEM((CHUNK_ROWS, width), jnp.bfloat16)] * len(plan),
        in_specs=[SMEM, SMEM] + [in_place] * 5,
        out_specs=[VMEM] * len(plan),
        scratch_shapes=[pltpu.SemaphoreType.DMA((len(plan) + fold - 1,))],
        compiler_params=pltpu.CompilerParams(vmem_limit_bytes=KERNEL_VMEM),
    )(
        publisher,
        version,
        *[
            pltpu.with_memory_space_constraint(x, pltpu.HBM)
            for x in (down, up_query, up_pair, out_down, out_up)
        ],
    )


def low_kernel(weight_ref, rows_ref, out_ref):
    out_ref[...] = lax.dot_general(
        rows_ref[...], weight_ref[...], CONTRACT_LAST, preferred_element_type=jnp.float32
    )


def out_low_kernel(weight_ref, rows_ref, out_ref):
    out_ref[...] = lax.dot_general(
        weight_ref[...], rows_ref[...], CONTRACT_LAST, preferred_element_type=jnp.float32
    )


def up_kernel(weight_ref, low_ref, out_ref):
    out_ref[...] = lax.dot_general(
        low_ref[...].astype(jnp.bfloat16),
        weight_ref[...],
        CONTRACT_FIRST,
        preferred_element_type=jnp.float32,
    ).astype(out_ref.dtype)


def pair_kernel(weight_ref, low_ref, keys_ref, values_ref, tables_ref, out_ref):
    width = keys_ref.shape[1]
    rank = ADAPTER_RANK
    fold = weight_ref.shape[1] // width
    rows = 2 * rank // fold
    up = jnp.concatenate(
        [weight_ref[:rows, i * width : (i + 1) * width] for i in range(fold)], axis=0
    )
    low = low_ref[...].astype(jnp.bfloat16)
    keys = keys_ref[...].astype(jnp.float32) + jnp.dot(
        low[:, :rank], up[:rank], preferred_element_type=jnp.float32
    )
    values = values_ref[...].astype(jnp.float32) + jnp.dot(
        low[:, rank:], up[rank:], preferred_element_type=jnp.float32
    )
    for head in range(0, width, HEAD_SIZE):
        out_ref[:, head : head + HEAD_SIZE] = rotate(
            keys[:, head : head + HEAD_SIZE], tables_ref[...]
        ).astype(jnp.bfloat16)
    out_ref[:, width:] = values.astype(jnp.bfloat16)


def attend_kernel(
    group_size, block_count, weight_ref, low_ref, base_ref, tables_ref, hidden_ref, *refs
):
    key_refs = refs[:block_count]
    value_refs = refs[block_count : 2 * block_count]
    out_ref = refs[-1]
    low = low_ref[...].astype(jnp.bfloat16)
    queries = base_ref[...].astype(jnp.float32) + jnp.dot(
        low, weight_ref[...], preferred_element_type=jnp.float32
    )
    group = None
    for lane in range(0, out_ref.shape[1], HEAD_SIZE):
        head = lane // HEAD_SIZE
        if head // group_size != group:
            group = head // group_size
            lanes = slice(group * HEAD_SIZE, (group + 1) * HEAD_SIZE)
            keys = jnp.concatenate([ref[:, lanes] for ref in key_refs], axis=0)
            values = jnp.concatenate([ref[:, lanes] for ref in value_refs], axis=0)
        turned = rotate(queries[:, lane : lane + HEAD_SIZE], tables_ref[...]).astype(jnp.bfloat16)
        scores = lax.dot_general(
            keys, turned, CONTRACT_LAST, preferred_element_type=jnp.float32
        )
        scores = scores + hidden_ref[...]
        raw = jnp.exp2((scores - jnp.max(scores, axis=0, keepdims=True)) * EXPONENT_SCALE)
        totals = jnp.sum(raw, axis=0, keepdims=True)
        mixed = lax.dot_general(
            values, raw.astype(jnp.bfloat16), CONTRACT_FIRST, preferred_element_type=jnp.float32
        )
        out_ref[:, lane : lane + HEAD_SIZE] = (mixed / totals).T.astype(jnp.bfloat16)


def token_positions(stored_block_order, first_row, row_count, half_rows):
    flat_index = first_row + jnp.arange(row_count, dtype=jnp.int32)
    block_index = flat_index // half_rows
    matches = (
        block_index[:, None] == jnp.arange(stored_block_order.shape[0], dtype=jnp.int32)[None, :]
    )
    stored_block = jnp.sum(jnp.where(matches, stored_block_order[None, :], 0), axis=1)
    return stored_block * half_rows + flat_index % half_rows


def shards(
    hidden,
    base_query_rows,
    base_key_rows,
    base_value_rows,
    stored_block_order,
    version,
    publisher,
    adapter_down_weight,
    adapter_up_query,
    adapter_up_key_value,
    output_down_weight,
    output_up_weight,
):
    rank = ADAPTER_RANK
    count = lax.axis_size("ctx")
    own_index = lax.axis_index("ctx")
    place = ring_place(own_index, count)
    pair_width = adapter_up_key_value.shape[-1]
    weights = (
        adapter_down_weight,
        adapter_up_query,
        adapter_up_key_value,
        output_down_weight,
        output_up_weight,
    )
    own = []
    for chunk_range in (slice(0, None),):
        own += own_chunks(chunk_range, publisher, version, *weights)
    per = rank // CHUNK_ROWS

    pairs = ring_pairs(count)
    arrived, sent = [], []
    for turn in range(LAG):
        sent.append(own[turn])
        arrived.append(lax.ppermute(own[turn], "ctx", pairs))
    source = after(publisher, *sent)[0]
    behind = (place - ring_place(source, count)) % count
    is_source = behind == 0
    for turn in range(LAG, len(own)):
        moving = after(arrived[turn - LAG], sent[-1])
        moving = jnp.where(is_source, own[turn], moving)
        sent.append(moving)
        arrived.append(lax.ppermute(moving, "ctx", pairs))
    late = []
    for turn in range(LAG * (count - 2) // JOINED):
        if turn < LAG // JOINED:
            first = len(own) - LAG + turn * JOINED
            moving = jnp.concatenate(arrived[first : first + JOINED], axis=0)
        else:
            moving = late[turn - LAG // JOINED]
        late.append(lax.ppermute(moving, "ctx", pairs))
    stored_block_order = after(stored_block_order, sent[3 * LAG])

    distance = jnp.full((1,), behind, jnp.int32)

    def on_chunks(kernel, first, number, operands, shape, dtype):
        chunks, candidates = {}, []
        for hop in range(-1, count - 1):
            held = []
            for k in range(first, first + number):
                turn = k + LAG * hop
                if hop < 0:
                    key, row, array = ("own", k), 0, own[k]
                elif turn < len(own):
                    key, row, array = ("ring", turn), 0, arrived[turn]
                else:
                    group, row = divmod(turn - len(own), JOINED)
                    key, row, array = ("late", group), row * CHUNK_ROWS, late[group]
                chunks[key] = array
                held.append((key, row))
            candidates.append(held)
        return chunk_call(
            kernel, distance, candidates, chunks, operands, jax.ShapeDtypeStruct(shape, dtype)
        )

    local_rows = hidden.shape[0]
    half_rows = local_rows // 2
    query_pos = token_positions(stored_block_order, own_index * local_rows, local_rows, half_rows)
    tables = rotation_tables(query_pos)

    part = on_chunks(low_kernel, 0, 2 * per, [hidden], (local_rows, 2 * rank), jnp.float32)
    pair_sums = doubling_sums(part, "tp", jnp.float32)
    part = on_chunks(low_kernel, 2 * per + 1, per, [hidden], (local_rows, rank), jnp.float32)
    query_sums = doubling_sums(part, "tp", jnp.float32)
    both = on_chunks(
        pair_kernel,
        2 * per,
        1,
        [pair_sums[-1], base_key_rows, base_value_rows, tables],
        (local_rows, 2 * pair_width),
        jnp.bfloat16,
    )

    forward, backward = ring_pairs(count), ring_pairs(count, back=True)
    key_blocks, value_blocks = {0: both[:, :pair_width]}, {0: both[:, pair_width:]}
    ahead, back = both, both
    for hop in range(1, (count - 1) // 2 + 1):
        ahead = lax.ppermute(ahead, "ctx", forward)
        back = lax.ppermute(back, "ctx", backward)
        for offset, block in ((-hop, ahead), (hop, back)):
            key_blocks[offset] = block[:, :pair_width]
            value_blocks[offset] = block[:, pair_width:]
    if count % 2 == 0:
        far = lax.ppermute(ahead[:, :pair_width], "ctx", forward)
        key_blocks[count // 2] = far
        far = lax.ppermute(back[:, pair_width:], "ctx", backward)
        value_blocks[count // 2] = far
    offsets = sorted(key_blocks)
    key_pos = jnp.concatenate(
        [
            token_positions(
                stored_block_order,
                ring_member((place + o) % count, count) * local_rows,
                local_rows,
                half_rows,
            )
            for o in offsets
        ]
    )
    hide = jnp.where(key_pos[:, None] <= query_pos[None, :], 0.0, NEG_BIG)
    local_heads = base_query_rows.shape[1] // HEAD_SIZE
    group_size = local_heads // (pair_width // HEAD_SIZE)
    attended = on_chunks(
        functools.partial(attend_kernel, group_size, len(offsets)),
        3 * per + 1,
        per,
        [query_sums[-1], base_query_rows, tables, hide]
        + [key_blocks[o] for o in offsets]
        + [value_blocks[o] for o in offsets],
        base_query_rows.shape,
        jnp.bfloat16,
    )
    part = on_chunks(out_low_kernel, 4 * per + 1, per, [attended], (rank, local_rows), jnp.float32)
    out_low = doubling_sums(part, "tp", jnp.bfloat16)[-1]
    adapted = on_chunks(up_kernel, 5 * per + 1, per, [out_low], attended.shape, jnp.bfloat16)
    return (attended, adapted)


def solution(mesh):
    placed = (
        P(("groups", "ctx"), "tp"),
        P(("groups", "ctx"), "tp"),
        P(("groups", "ctx"), "tp"),
        P(("groups", "ctx"), "tp"),
        P("groups"),
        P("groups"),
        P("groups"),
        P("ctx", None, None, "tp"),
        P("ctx", None, None, "tp"),
        P("ctx", None, None, None, "tp"),
        P("ctx", None, None, "tp"),
        P("ctx", None, None, "tp"),
    )
    return jax.shard_map(
        shards,
        mesh=mesh,
        in_specs=placed,
        out_specs=(P(("groups", "ctx"), "tp"), P(("groups", "ctx"), "tp")),
        check_vma=False,
    )
```

```python
import functools
import math

import jax
import jax.numpy as jnp
from jax import lax
from jax.experimental import pallas as pl
from jax.experimental.pallas import tpu as pltpu
from jax.sharding import PartitionSpec as P


HEAD_SIZE = 128
ADAPTER_RANK = 64
NEG_BIG = -1e30
EXPONENT_SCALE = HEAD_SIZE ** (-0.5) * math.log2(math.e)
CHUNK_ROWS = 16
LAG = 4
JOINED = 2
UP_BLOCKS = 4
KERNEL_VMEM = 8 << 20


def after(value, *earlier):
    return lax.optimization_barrier((value,) + earlier)[0]


def ring_order(count):
    return [0] + list(range(1, count, 2)) + list(range(2, count, 2))[::-1]


def ring_place(index, count):
    table = [0] * count
    for place, member in enumerate(ring_order(count)):
        table[member] = place
    place = jnp.int32(0)
    for member in range(count):
        place = jnp.where(index == member, table[member], place)
    return place


def ring_member(place, count):
    member = jnp.int32(0)
    for at, who in enumerate(ring_order(count)):
        member = jnp.where(place == at, who, member)
    return member


def ring_pairs(count, back=False):
    order = ring_order(count)
    pairs = [(order[i], order[(i + 1) % count]) for i in range(count)]
    return [(b, a) for a, b in pairs] if back else pairs


def doubling_sums(value, axis, wire):
    count = lax.axis_size(axis)
    if count & (count - 1):
        return [lax.psum(value, axis)]
    sums = []
    step = 1
    while step < count:
        pairs = [(i, i ^ step) for i in range(count)]
        sent = value.astype(wire)
        other = lax.ppermute(sent, axis, pairs)
        value = sent.astype(jnp.float32) + other.astype(jnp.float32)
        sums.append(value)
        step *= 2
    return sums


def rotation_tables(token_index_list):
    half_dim = HEAD_SIZE // 2
    frequency = 500000.0 ** (-(jnp.arange(half_dim, dtype=jnp.float32) * 2.0) / HEAD_SIZE)
    angles = token_index_list.astype(jnp.float32)[:, None] * frequency[None, :]
    cosine, sine = jnp.cos(angles), jnp.sin(angles)
    return jnp.concatenate([cosine, cosine, -sine, sine], axis=1)


def rotate(values, tables):
    swapped = pltpu.roll(values, HEAD_SIZE // 2, axis=1)
    return values * tables[:, :HEAD_SIZE] + swapped * tables[:, HEAD_SIZE:]


CONTRACT_LAST = (((1,), (1,)), ((), ()))
CONTRACT_FIRST = (((0,), (0,)), ((), ()))
VMEM = pl.BlockSpec(memory_space=pltpu.VMEM)
SMEM = pl.BlockSpec(memory_space=pltpu.SMEM)


def chunk_call(kernel, behind, candidates, chunks, operands, out_shape, scratch=()):
    names = sorted(chunks)
    rows, width = CHUNK_ROWS, chunks[names[0]].shape[1]
    number = len(candidates[0])

    def body(behind_ref, *refs):
        chunk_refs = dict(zip(names, refs))
        weight_ref = refs[len(names) + len(operands) + 1]
        for distance, held in enumerate(candidates):

            @pl.when(behind_ref[0] == distance)
            def _(held=held):
                for i, (name, row) in enumerate(held):
                    weight_ref[i * rows : (i + 1) * rows, :] = chunk_refs[name][row : row + rows]

        last = len(names) + len(operands) + 1
        kernel(weight_ref, *refs[len(names) : last], *refs[last + 1 :])

    return pl.pallas_call(
        body,
        out_shape=out_shape if scratch else pltpu.VMEM(out_shape.shape, out_shape.dtype),
        in_specs=[SMEM] + [VMEM] * (len(names) + len(operands)),
        out_specs=pl.BlockSpec(memory_space=pltpu.HBM) if scratch else VMEM,
        scratch_shapes=[pltpu.VMEM((number * rows, width), jnp.bfloat16), *scratch],
        compiler_params=pltpu.CompilerParams(vmem_limit_bytes=KERNEL_VMEM),
    )(
        behind,
        *[
            pltpu.with_memory_space_constraint(x, pltpu.VMEM)
            for x in [chunks[name] for name in names] + operands
        ],
    )


def own_chunks(chunk_range, publisher, version, down, up_query, up_pair, out_down, out_up):
    rank = ADAPTER_RANK
    width = down.shape[-1]
    pair_width = up_pair.shape[-1]
    fold = width // pair_width
    pair_rows = 2 * rank // fold
    plan = [(0, rank + first) for first in range(0, 2 * rank, CHUNK_ROWS)] + [(2, 0)]
    plan += [(0, first) for first in range(0, rank, CHUNK_ROWS)]
    for weight in (1, 3, 4):
        plan += [(weight, first) for first in range(0, rank, CHUNK_ROWS)]
    plan = plan[chunk_range]

    def body(publisher_ref, version_ref, *refs):
        weights, outs, sem = refs[:5], refs[5:-1], refs[-1]
        chosen = version_ref[publisher_ref[0]]
        copies = []
        for (which, first), out in zip(plan, outs):
            if which != 2:
                rows = weights[which].at[0, chosen, pl.ds(first, CHUNK_ROWS)]
                copies.append((rows, out))
                continue
            for i in range(fold):
                half, row = divmod(i * pair_rows, rank)
                rows = weights[which].at[0, chosen, half, pl.ds(row, pair_rows)]
                lanes = pl.ds(i * pair_width, pair_width)
                copies.append((rows, out.at[pl.ds(0, pair_rows), lanes]))
        copies = [
            pltpu.make_async_copy(rows, out, sem.at[i]) for i, (rows, out) in enumerate(copies)
        ]
        for copy in copies:
            copy.start()
        for copy in copies:
            copy.wait()

    in_place = pl.BlockSpec(memory_space=pltpu.HBM)
    return pl.pallas_call(
        body,
        out_shape=[pltpu.VMEM((CHUNK_ROWS, width), jnp.bfloat16)] * len(plan),
        in_specs=[SMEM, SMEM] + [in_place] * 5,
        out_specs=[VMEM] * len(plan),
        scratch_shapes=[pltpu.SemaphoreType.DMA((len(plan) + fold - 1,))],
        compiler_params=pltpu.CompilerParams(vmem_limit_bytes=KERNEL_VMEM),
    )(
        publisher,
        version,
        *[
            pltpu.with_memory_space_constraint(x, pltpu.HBM)
            for x in (down, up_query, up_pair, out_down, out_up)
        ],
    )


def low_kernel(weight_ref, rows_ref, out_ref):
    out_ref[...] = lax.dot_general(
        rows_ref[...], weight_ref[...], CONTRACT_LAST, preferred_element_type=jnp.float32
    )


def out_low_kernel(weight_ref, rows_ref, out_ref):
    out_ref[...] = lax.dot_general(
        weight_ref[...], rows_ref[...], CONTRACT_LAST, preferred_element_type=jnp.float32
    )


def up_kernel(weight_ref, low_ref, out_hbm, rows_ref, sem):
    low = low_ref[...].astype(jnp.bfloat16)
    step = rows_ref.shape[1] // UP_BLOCKS
    copies = []
    for block in range(UP_BLOCKS):
        lanes = pl.ds(block * step, step)
        rows_ref[:, lanes] = lax.dot_general(
            low, weight_ref[:, lanes], CONTRACT_FIRST, preferred_element_type=jnp.float32
        ).astype(rows_ref.dtype)
        copy = pltpu.make_async_copy(rows_ref.at[:, lanes], out_hbm.at[:, lanes], sem.at[block])
        copy.start()
        copies.append(copy)
    for copy in copies:
        copy.wait()


def pair_kernel(weight_ref, low_ref, keys_ref, values_ref, tables_ref, out_ref):
    width = keys_ref.shape[1]
    rank = ADAPTER_RANK
    fold = weight_ref.shape[1] // width
    rows = 2 * rank // fold
    up = jnp.concatenate(
        [weight_ref[:rows, i * width : (i + 1) * width] for i in range(fold)], axis=0
    )
    low = low_ref[...].astype(jnp.bfloat16)
    keys = keys_ref[...].astype(jnp.float32) + jnp.dot(
        low[:, :rank], up[:rank], preferred_element_type=jnp.float32
    )
    values = values_ref[...].astype(jnp.float32) + jnp.dot(
        low[:, rank:], up[rank:], preferred_element_type=jnp.float32
    )
    for head in range(0, width, HEAD_SIZE):
        out_ref[:, head : head + HEAD_SIZE] = rotate(
            keys[:, head : head + HEAD_SIZE], tables_ref[...]
        ).astype(jnp.bfloat16)
    out_ref[:, width:] = values.astype(jnp.bfloat16)


def query_kernel(weight_ref, low_ref, base_ref, tables_ref, out_ref):
    low = low_ref[...].astype(jnp.bfloat16)
    queries = base_ref[...].astype(jnp.float32) + jnp.dot(
        low, weight_ref[...], preferred_element_type=jnp.float32
    )
    for lane in range(0, out_ref.shape[1], HEAD_SIZE):
        out_ref[:, lane : lane + HEAD_SIZE] = rotate(
            queries[:, lane : lane + HEAD_SIZE], tables_ref[...]
        ).astype(jnp.bfloat16)


def attend_kernel(group_size, block_count, queries_ref, hidden_ref, *refs):
    key_refs = refs[:block_count]
    value_refs = refs[block_count : 2 * block_count]
    out_ref = refs[-1]
    group = None
    for lane in range(0, out_ref.shape[1], HEAD_SIZE):
        head = lane // HEAD_SIZE
        if head // group_size != group:
            group = head // group_size
            lanes = slice(group * HEAD_SIZE, (group + 1) * HEAD_SIZE)
            keys = jnp.concatenate([ref[:, lanes] for ref in key_refs], axis=0)
            values = jnp.concatenate([ref[:, lanes] for ref in value_refs], axis=0)
        turned = queries_ref[:, lane : lane + HEAD_SIZE]
        scores = lax.dot_general(
            keys, turned, CONTRACT_LAST, preferred_element_type=jnp.float32
        )
        scores = scores + hidden_ref[...]
        raw = jnp.exp2((scores - jnp.max(scores, axis=0, keepdims=True)) * EXPONENT_SCALE)
        totals = jnp.sum(raw, axis=0, keepdims=True)
        mixed = lax.dot_general(
            values, raw.astype(jnp.bfloat16), CONTRACT_FIRST, preferred_element_type=jnp.float32
        )
        out_ref[:, lane : lane + HEAD_SIZE] = (mixed / totals).T.astype(jnp.bfloat16)


def token_positions(stored_block_order, first_row, row_count, half_rows):
    flat_index = first_row + jnp.arange(row_count, dtype=jnp.int32)
    block_index = flat_index // half_rows
    matches = (
        block_index[:, None] == jnp.arange(stored_block_order.shape[0], dtype=jnp.int32)[None, :]
    )
    stored_block = jnp.sum(jnp.where(matches, stored_block_order[None, :], 0), axis=1)
    return stored_block * half_rows + flat_index % half_rows


def shards(
    hidden,
    base_query_rows,
    base_key_rows,
    base_value_rows,
    stored_block_order,
    version,
    publisher,
    adapter_down_weight,
    adapter_up_query,
    adapter_up_key_value,
    output_down_weight,
    output_up_weight,
):
    rank = ADAPTER_RANK
    count = lax.axis_size("ctx")
    own_index = lax.axis_index("ctx")
    place = ring_place(own_index, count)
    pair_width = adapter_up_key_value.shape[-1]
    weights = (
        adapter_down_weight,
        adapter_up_query,
        adapter_up_key_value,
        output_down_weight,
        output_up_weight,
    )
    own = []
    for chunk_range in (slice(0, None),):
        own += own_chunks(chunk_range, publisher, version, *weights)
    per = rank // CHUNK_ROWS

    pairs = ring_pairs(count)
    arrived, sent = [], []
    for turn in range(LAG):
        sent.append(own[turn])
        arrived.append(lax.ppermute(own[turn], "ctx", pairs))
    source = after(publisher, *sent)[0]
    behind = (place - ring_place(source, count)) % count
    is_source = behind == 0
    for turn in range(LAG, len(own)):
        moving = after(arrived[turn - LAG], sent[-1])
        moving = jnp.where(is_source, own[turn], moving)
        sent.append(moving)
        arrived.append(lax.ppermute(moving, "ctx", pairs))
    late = []
    for turn in range(LAG * (count - 2) // JOINED):
        if turn < LAG // JOINED:
            first = len(own) - LAG + turn * JOINED
            moving = jnp.concatenate(arrived[first : first + JOINED], axis=0)
        else:
            moving = late[turn - LAG // JOINED]
        late.append(lax.ppermute(moving, "ctx", pairs))
    stored_block_order = after(stored_block_order, sent[3 * LAG])

    distance = jnp.full((1,), behind, jnp.int32)

    def on_chunks(kernel, first, number, operands, shape, dtype, scratch=()):
        chunks, candidates = {}, []
        for hop in range(-1, count - 1):
            held = []
            for k in range(first, first + number):
                turn = k + LAG * hop
                if hop < 0:
                    key, row, array = ("own", k), 0, own[k]
                elif turn < len(own):
                    key, row, array = ("ring", turn), 0, arrived[turn]
                else:
                    group, row = divmod(turn - len(own), JOINED)
                    key, row, array = ("late", group), row * CHUNK_ROWS, late[group]
                chunks[key] = array
                held.append((key, row))
            candidates.append(held)
        return chunk_call(
            kernel,
            distance,
            candidates,
            chunks,
            operands,
            jax.ShapeDtypeStruct(shape, dtype),
            scratch,
        )

    local_rows = hidden.shape[0]
    half_rows = local_rows // 2
    query_pos = token_positions(stored_block_order, own_index * local_rows, local_rows, half_rows)
    tables = rotation_tables(query_pos)

    part = on_chunks(low_kernel, 0, 2 * per, [hidden], (local_rows, 2 * rank), jnp.float32)
    pair_sums = doubling_sums(part, "tp", jnp.float32)
    part = on_chunks(low_kernel, 2 * per + 1, per, [hidden], (local_rows, rank), jnp.float32)
    query_sums = doubling_sums(part, "tp", jnp.float32)
    both = on_chunks(
        pair_kernel,
        2 * per,
        1,
        [pair_sums[-1], base_key_rows, base_value_rows, tables],
        (local_rows, 2 * pair_width),
        jnp.bfloat16,
    )

    forward, backward = ring_pairs(count), ring_pairs(count, back=True)
    key_blocks, value_blocks = {0: both[:, :pair_width]}, {0: both[:, pair_width:]}
    ahead, back = both, both
    for hop in range(1, (count - 1) // 2 + 1):
        ahead = lax.ppermute(ahead, "ctx", forward)
        back = lax.ppermute(back, "ctx", backward)
        for offset, block in ((-hop, ahead), (hop, back)):
            key_blocks[offset] = block[:, :pair_width]
            value_blocks[offset] = block[:, pair_width:]
    if count % 2 == 0:
        far = lax.ppermute(ahead[:, :pair_width], "ctx", forward)
        key_blocks[count // 2] = far
        far = lax.ppermute(back[:, pair_width:], "ctx", backward)
        value_blocks[count // 2] = far
    offsets = sorted(key_blocks)
    key_pos = jnp.concatenate(
        [
            token_positions(
                stored_block_order,
                ring_member((place + o) % count, count) * local_rows,
                local_rows,
                half_rows,
            )
            for o in offsets
        ]
    )
    hide = jnp.where(key_pos[:, None] <= query_pos[None, :], 0.0, NEG_BIG)
    local_heads = base_query_rows.shape[1] // HEAD_SIZE
    group_size = local_heads // (pair_width // HEAD_SIZE)
    queries = on_chunks(
        query_kernel,
        3 * per + 1,
        per,
        [query_sums[-1], base_query_rows, tables],
        base_query_rows.shape,
        jnp.bfloat16,
    )
    operands = [queries, hide]
    operands += [key_blocks[o] for o in offsets] + [value_blocks[o] for o in offsets]
    attended = pl.pallas_call(
        functools.partial(attend_kernel, group_size, len(offsets)),
        out_shape=pltpu.VMEM(queries.shape, jnp.bfloat16),
        in_specs=[VMEM] * len(operands),
        out_specs=VMEM,
        compiler_params=pltpu.CompilerParams(vmem_limit_bytes=KERNEL_VMEM),
    )(*[pltpu.with_memory_space_constraint(x, pltpu.VMEM) for x in operands])
    part = on_chunks(out_low_kernel, 4 * per + 1, per, [attended], (rank, local_rows), jnp.float32)
    out_low = doubling_sums(part, "tp", jnp.bfloat16)[-1]
    adapted = on_chunks(
        up_kernel,
        5 * per + 1,
        per,
        [out_low],
        attended.shape,
        jnp.bfloat16,
        (
            pltpu.VMEM(attended.shape, jnp.bfloat16),
            pltpu.SemaphoreType.DMA((UP_BLOCKS,)),
        ),
    )
    return (attended, adapted)


def solution(mesh):
    placed = (
        P(("groups", "ctx"), "tp"),
        P(("groups", "ctx"), "tp"),
        P(("groups", "ctx"), "tp"),
        P(("groups", "ctx"), "tp"),
        P("groups"),
        P("groups"),
        P("groups"),
        P("ctx", None, None, "tp"),
        P("ctx", None, None, "tp"),
        P("ctx", None, None, None, "tp"),
        P("ctx", None, None, "tp"),
        P("ctx", None, None, "tp"),
    )
    return jax.shard_map(
        shards,
        mesh=mesh,
        in_specs=placed,
        out_specs=(P(("groups", "ctx"), "tp"), P(("groups", "ctx"), "tp")),
        check_vma=False,
    )
```
